32 devices in a mesh: row: 8 (over z, y), col: 4 (over x, core).
Axes of the slice: x: 2, y: 2, z: 4, core: 2. Of those that a mesh axis runs over, the one named last changes fastest.
Arguments:
- embeddings: bfloat16 [512, 1024], P(('row', 'col')), may hold values from -20 to 20
- group_ids: int32 [512], P(('row', 'col')), may hold values from 0 to 127, as said below
Outputs:
- loss: float32 [], replicated
- grad: bfloat16 [512, 1024], P(('row', 'col'))
The draws below stay inside these ranges and needn't reach their ends.
Inputs may be any that keep to these rules, and one draw needn't show every extreme that they name: `group_ids`: every group id is held by exactly 4 rows, spread over the batch.
All inputs are finite; a program needn't handle non-finite values.
Results may differ from the reference program's by a relative error of at most 0.0045.
Values may be sent and summed in bfloat16 or wider, within the bound.
No kernel may reach another device: no remote copies, remote signals or barrier semaphores. Data moves between devices by JAX's collectives and lax.ppermute only.
A program may use at most 64 MiB of HBM per device.

```python
import jax
import jax.numpy as jnp
from jax import lax

D = 1024
GROUP = 4
N = 512
N_ROW = 8


def draw_embeddings(key, part):
    values = jnp.clip(jax.random.normal(key, (N, D), jnp.float32), -6.0, 6.0)
    signs = jnp.where(jax.random.bernoulli(jax.random.fold_in(key, 11), 0.5, (D,)), 1.0, -1.0).astype(jnp.float32)
    index = jnp.arange(N)
    blocks = index // 64
    within = index % 64
    target = 100.0 + 80.0 * (blocks % 4).astype(jnp.float32) + 1.5 * within.astype(jnp.float32)
    strength = jnp.sqrt(target / jnp.sqrt(jnp.float32(D)))
    aligned = within < 3
    values = jnp.where(aligned[:, None], strength[:, None] * signs[None, :], values)
    return values.astype(jnp.bfloat16)


def draw_group_ids(key, part):
    order = jax.random.permutation(key, N)
    return (order // GROUP).astype(jnp.int32)


def setup_inputs(seed: int = 0) -> dict:
    keys = jax.random.split(jax.random.key(seed), 3)
    embeddings = draw_embeddings(jax.random.fold_in(keys[2], 71), 0)
    group_ids = draw_group_ids(jax.random.fold_in(keys[2], 71), 0)
    return dict(embeddings=embeddings, group_ids=group_ids)


def reference(embeddings, group_ids):
    scale = 1.0 / jnp.sqrt(jnp.float32(D))
    block = N // N_ROW
    starts = jnp.arange(N_ROW, dtype=jnp.int32) * block
    every = jnp.arange(N, dtype=jnp.int32)

    def tile(start):
        queries = lax.dynamic_slice_in_dim(embeddings, start, block, 0)
        query_groups = lax.dynamic_slice_in_dim(group_ids, start, block, 0)
        index = start + jnp.arange(block, dtype=jnp.int32)
        scores = lax.dot_general(queries, embeddings, (((1,), (1,)), ((), ())), preferred_element_type=jnp.float32) * scale
        selfs = index[:, None] == every[None, :]
        positive = jnp.logical_and(query_groups[:, None] == group_ids[None, :], jnp.logical_not(selfs))
        masked = jnp.where(selfs, jnp.float32(-1e+30), scores)
        return (queries, scores, masked, positive)

    def stats(start):
        queries, scores, masked, positive = tile(start)
        peak = lax.optimization_barrier(jnp.max(masked, axis=1))
        total = lax.optimization_barrier(jnp.sum(jnp.exp(masked - peak[:, None]), axis=1))
        lse = peak + jnp.log(total)
        possum = lax.optimization_barrier(jnp.sum(jnp.where(positive, scores, jnp.float32(0.0)), axis=1))
        count = lax.optimization_barrier(jnp.sum(positive.astype(jnp.float32), axis=1))
        return (lse, possum, count)
    lse, possum, count = lax.map(stats, starts)
    lse = lse.reshape(N)
    possum = possum.reshape(N)
    count = count.reshape(N)
    loss = jnp.sum(lse - possum / count) / N

    def grads(carry, start):
        queries, scores, masked, positive = tile(start)
        block_lse = lax.dynamic_slice_in_dim(lse, start, block, 0)
        block_inv = 1.0 / lax.dynamic_slice_in_dim(count, start, block, 0)
        weight = (jnp.exp(masked - block_lse[:, None]) - jnp.where(positive, block_inv[:, None], jnp.float32(0.0))) / N
        weight = weight.astype(jnp.bfloat16)
        carry = carry + lax.dot_general(weight, queries, (((0,), (0,)), ((), ())), preferred_element_type=jnp.float32)
        rows_part = jnp.dot(weight, embeddings, preferred_element_type=jnp.float32)
        return (carry, rows_part)
    cols_part, rows_part = lax.scan(grads, jnp.zeros((N, D), jnp.float32), starts)
    grad = (scale * (rows_part.reshape(N, D) + cols_part)).astype(jnp.bfloat16)
    return (loss, grad)
```

```python
import jax
import jax.numpy as jnp
from jax import lax
from jax.experimental import pallas as pl
from jax.experimental.pallas import tpu as pltpu
from jax.sharding import PartitionSpec as P

AXES = ("row", "col")
LANES = 128
RADIX = 256


def stage_bits(bits, parity):
    far = [b for b in range(bits) if b >= 3]
    near = [b for b in (1, 2) if b < bits]
    return far + (near if parity == 0 else near[::-1]) + [0]


def swap_pairs(devices, stage):
    bits = devices.bit_length() - 1
    return [(i, i ^ (1 << stage_bits(bits, i & 1)[stage])) for i in range(devices)]


def loss_and_grad(width, own_ref, near_ref, far_ref, loss_ref, grad_ref, lse_ref, inv_ref):
    own = own_ref.shape[0]
    half = near_ref.shape[0]
    total = 2 * half
    block = min(half, 256)
    scale = 1.0 / jnp.sqrt(jnp.float32(width))
    refs = (near_ref, far_ref)
    nt = (((1,), (1,)), ((), ()))

    def dot_nt(a, b):
        return lax.dot_general(a, b, nt, preferred_element_type=jnp.float32)

    lane = lax.broadcasted_iota(jnp.int32, (block, LANES), 1)
    pick = jnp.where(lane == 0, 1.0, jnp.where(lane == 1, float(RADIX), 0.0)).astype(jnp.bfloat16)

    def block_stats(side, start, loss):
        cols = refs[side][pl.ds(start, block), :width]
        col_ids = dot_nt(pick[:16], refs[side][pl.ds(start, block), width:])[:1]
        col_pos = side * half + start + lax.broadcasted_iota(jnp.int32, (block, block), 1)
        parts = []
        for other in range(2):
            for first in range(0, half, block):
                rows = refs[other][first : first + block, :width]
                s = dot_nt(rows, cols) * scale
                row_ids = dot_nt(refs[other][first : first + block, width:], pick)
                row_pos = other * half + first + lax.broadcasted_iota(jnp.int32, (block, block), 0)
                selfs = row_pos == col_pos
                positive = jnp.logical_and(row_ids == col_ids, jnp.logical_not(selfs))
                masked = jnp.where(selfs, jnp.float32(-1e30), s)
                top = jnp.max(masked, axis=0, keepdims=True)
                add = jnp.sum(jnp.exp(masked - top), axis=0, keepdims=True)
                possum = jnp.sum(jnp.where(positive, s, 0.0), axis=0, keepdims=True)
                count = jnp.sum(positive.astype(jnp.float32), axis=0, keepdims=True)
                parts.append((top, add, possum, count))
        peak = parts[0][0]
        for p in parts[1:]:
            peak = jnp.maximum(peak, p[0])
        added = sum(p[1] * jnp.exp(p[0] - peak) for p in parts)
        possum = sum(p[2] for p in parts)
        inverse = 1.0 / sum(p[3] for p in parts)
        lse = peak + jnp.log(added)
        at = pl.ds(side * half + start, block)
        lse_ref[:, at] = lse
        inv_ref[:, at] = inverse
        return loss + jnp.sum(lse - possum * inverse)

    loss = jnp.float32(0.0)
    for side in range(2):
        steps = half // block
        if steps == 1:
            loss = block_stats(side, 0, loss)
        else:
            loss = lax.fori_loop(
                0, steps, lambda k, v: block_stats(side, pl.multiple_of(k * block, block), v), loss
            )
    loss_ref[0] = loss / total

    mine = own_ref[:, :width]
    own_ids = dot_nt(own_ref[:, width:], pick[:LANES])[:, :1]
    out = jnp.zeros((2 * own, width), jnp.float32)
    s, positive = [], []
    for other in range(2):
        s.append(dot_nt(mine, refs[other][:, :width]) * scale)
        ids = dot_nt(pick[:16], refs[other][:, width:])[:1]
        positive.append(own_ids == ids)
    s = jnp.concatenate(s, axis=1)
    positive = jnp.concatenate(positive, axis=1)
    selfs = lax.broadcasted_iota(jnp.int32, s.shape, 0) == lax.broadcasted_iota(jnp.int32, s.shape, 1)
    positive = jnp.logical_and(positive, jnp.logical_not(selfs))
    masked = jnp.where(selfs, jnp.float32(-1e30), s)
    peak = jnp.max(masked, axis=1, keepdims=True)
    lse = peak + jnp.log(jnp.sum(jnp.exp(masked - peak), axis=1, keepdims=True))
    inverse = 1.0 / jnp.sum(positive.astype(jnp.float32), axis=1, keepdims=True)
    weight = (jnp.exp(masked - lse) - jnp.where(positive, inverse, 0.0)) / total
    mirrored = (jnp.exp(masked - lse_ref[...]) - jnp.where(positive, inv_ref[...], 0.0)) / total
    both = jnp.concatenate([weight, mirrored], axis=0).astype(jnp.bfloat16)
    for other in range(2):
        out += jnp.dot(
            both[:, other * half : (other + 1) * half],
            refs[other][:, :width],
            preferred_element_type=jnp.float32,
        )
    grad_ref[...] = (scale * (out[:own] + out[own:])).astype(jnp.bfloat16)


def on_device(devices, embeddings, group_ids):
    rows, width = embeddings.shape
    bits = devices.bit_length() - 1
    lane = lax.broadcasted_iota(jnp.int32, (rows, LANES), 1)
    ids = group_ids[:, None]
    coded = jnp.where(lane == 0, ids % RADIX, jnp.where(lane == 1, ids // RADIX, 0))
    held = jnp.concatenate([embeddings, coded.astype(jnp.bfloat16)], axis=1)
    own = held
    for stage in range(bits):
        came = lax.ppermute(held, AXES, swap_pairs(devices, stage))
        if stage < bits - 1:
            held = jnp.concatenate([held, came], axis=0)
    total = rows * devices
    vmem = pl.BlockSpec(memory_space=pltpu.VMEM)
    loss, grad = pl.pallas_call(
        lambda *refs: loss_and_grad(width, *refs),
        out_shape=(
            jax.ShapeDtypeStruct((1,), jnp.float32),
            jax.ShapeDtypeStruct((rows, width), jnp.bfloat16),
        ),
        in_specs=[vmem, vmem, vmem],
        out_specs=(pl.BlockSpec(memory_space=pltpu.SMEM), vmem),
        scratch_shapes=[pltpu.VMEM((1, total), jnp.float32), pltpu.VMEM((1, total), jnp.float32)],
        cost_estimate=pl.CostEstimate(
            flops=2 * total * total * width, bytes_accessed=2 * total * width, transcendentals=total * total
        ),
    )(own, held, came)
    return (loss[0], grad)


def solution(mesh):
    in_specs = (P(AXES, None), P(AXES))
    out_specs = (P(), P(AXES, None))
    devices = mesh.shape["row"] * mesh.shape["col"]

    def body(embeddings, group_ids):
        return on_device(devices, embeddings, group_ids)

    return jax.shard_map(body, mesh=mesh, in_specs=in_specs, out_specs=out_specs, check_vma=False)
```

```python
import jax
import jax.numpy as jnp
from jax import lax
from jax.experimental import pallas as pl
from jax.experimental.pallas import tpu as pltpu
from jax.sharding import PartitionSpec as P

AXES = ("row", "col")
LANES = 128
RADIX = 256


def phases(bits):
    far = [b for b in range(bits) if b >= 3]
    near = [b for b in (1, 2) if b < bits]
    return [far[k : k + 2] for k in range(0, len(far), 2)] + [near, [0]]


def exchange(devices, group, held):
    masks = [0]
    for b in group:
        masks += [m | (1 << b) for m in masks]
    return [held] + [lax.ppermute(held, AXES, [(i, i ^ m) for i in range(devices)]) for m in masks[1:]]


def loss_and_grad(width, own_ref, near_ref, far_ref, loss_ref, grad_ref, lse_ref, inv_ref):
    own = own_ref.shape[0]
    half = near_ref.shape[0]
    total = 2 * half
    block = min(half, 256)
    scale = 1.0 / jnp.sqrt(jnp.float32(width))
    refs = (near_ref, far_ref)
    nt = (((1,), (1,)), ((), ()))

    def dot_nt(a, b):
        return lax.dot_general(a, b, nt, preferred_element_type=jnp.float32)

    lane = lax.broadcasted_iota(jnp.int32, (block, LANES), 1)
    pick = jnp.where(lane == 0, 1.0, jnp.where(lane == 1, float(RADIX), 0.0)).astype(jnp.bfloat16)

    def block_stats(side, start, loss):
        cols = refs[side][pl.ds(start, block), :width]
        col_ids = dot_nt(pick[:16], refs[side][pl.ds(start, block), width:])[:1]
        col_pos = side * half + start + lax.broadcasted_iota(jnp.int32, (block, block), 1)
        parts = []
        for other in range(2):
            for first in range(0, half, block):
                rows = refs[other][first : first + block, :width]
                s = dot_nt(rows, cols) * scale
                row_ids = dot_nt(refs[other][first : first + block, width:], pick)
                row_pos = other * half + first + lax.broadcasted_iota(jnp.int32, (block, block), 0)
                selfs = row_pos == col_pos
                positive = jnp.logical_and(row_ids == col_ids, jnp.logical_not(selfs))
                masked = jnp.where(selfs, jnp.float32(-1e30), s)
                top = jnp.max(masked, axis=0, keepdims=True)
                add = jnp.sum(jnp.exp(masked - top), axis=0, keepdims=True)
                possum = jnp.sum(jnp.where(positive, s, 0.0), axis=0, keepdims=True)
                count = jnp.sum(positive.astype(jnp.float32), axis=0, keepdims=True)
                parts.append((top, add, possum, count))
        peak = parts[0][0]
        for p in parts[1:]:
            peak = jnp.maximum(peak, p[0])
        added = sum(p[1] * jnp.exp(p[0] - peak) for p in parts)
        possum = sum(p[2] for p in parts)
        inverse = 1.0 / sum(p[3] for p in parts)
        lse = peak + jnp.log(added)
        at = pl.ds(side * half + start, block)
        lse_ref[:, at] = lse
        inv_ref[:, at] = inverse
        return loss + jnp.sum(lse - possum * inverse)

    loss = jnp.float32(0.0)
    for side in range(2):
        steps = half // block
        if steps == 1:
            loss = block_stats(side, 0, loss)
        else:
            loss = lax.fori_loop(
                0, steps, lambda k, v: block_stats(side, pl.multiple_of(k * block, block), v), loss
            )
    loss_ref[0] = loss / total

    mine = own_ref[:, :width]
    own_ids = dot_nt(own_ref[:, width:], pick[:LANES])[:, :1]
    out = jnp.zeros((2 * own, width), jnp.float32)
    s, positive = [], []
    for other in range(2):
        s.append(dot_nt(mine, refs[other][:, :width]) * scale)
        ids = dot_nt(pick[:16], refs[other][:, width:])[:1]
        positive.append(own_ids == ids)
    s = jnp.concatenate(s, axis=1)
    positive = jnp.concatenate(positive, axis=1)
    selfs = lax.broadcasted_iota(jnp.int32, s.shape, 0) == lax.broadcasted_iota(jnp.int32, s.shape, 1)
    positive = jnp.logical_and(positive, jnp.logical_not(selfs))
    masked = jnp.where(selfs, jnp.float32(-1e30), s)
    peak = jnp.max(masked, axis=1, keepdims=True)
    lse = peak + jnp.log(jnp.sum(jnp.exp(masked - peak), axis=1, keepdims=True))
    inverse = 1.0 / jnp.sum(positive.astype(jnp.float32), axis=1, keepdims=True)
    weight = (jnp.exp(masked - lse) - jnp.where(positive, inverse, 0.0)) / total
    mirrored = (jnp.exp(masked - lse_ref[...]) - jnp.where(positive, inv_ref[...], 0.0)) / total
    both = jnp.concatenate([weight, mirrored], axis=0).astype(jnp.bfloat16)
    for other in range(2):
        out += jnp.dot(
            both[:, other * half : (other + 1) * half],
            refs[other][:, :width],
            preferred_element_type=jnp.float32,
        )
    grad_ref[...] = (scale * (out[:own] + out[own:])).astype(jnp.bfloat16)


def on_device(devices, embeddings, group_ids):
    rows, width = embeddings.shape
    bits = devices.bit_length() - 1
    lane = lax.broadcasted_iota(jnp.int32, (rows, LANES), 1)
    ids = group_ids[:, None]
    coded = jnp.where(lane == 0, ids % RADIX, jnp.where(lane == 1, ids // RADIX, 0))
    held = jnp.concatenate([embeddings, coded.astype(jnp.bfloat16)], axis=1)
    own = held
    for group in phases(bits)[:-1]:
        held = jnp.concatenate(exchange(devices, group, held), axis=0)
    held, came = exchange(devices, [0], held)
    total = rows * devices
    vmem = pl.BlockSpec(memory_space=pltpu.VMEM)
    loss, grad = pl.pallas_call(
        lambda *refs: loss_and_grad(width, *refs),
        out_shape=(
            jax.ShapeDtypeStruct((1,), jnp.float32),
            jax.ShapeDtypeStruct((rows, width), jnp.bfloat16),
        ),
        in_specs=[vmem, vmem, vmem],
        out_specs=(pl.BlockSpec(memory_space=pltpu.SMEM), vmem),
        scratch_shapes=[pltpu.VMEM((1, total), jnp.float32), pltpu.VMEM((1, total), jnp.float32)],
        compiler_params=pltpu.CompilerParams(vmem_limit_bytes=(8 << 20) + 8 * total * width),
        cost_estimate=pl.CostEstimate(
            flops=2 * total * total * width, bytes_accessed=2 * total * width, transcendentals=total * total
        ),
    )(own, held, came)
    return (loss[0], grad)


def solution(mesh):
    in_specs = (P(AXES, None), P(AXES))
    out_specs = (P(), P(AXES, None))
    devices = mesh.shape["row"] * mesh.shape["col"]

    def body(embeddings, group_ids):
        return on_device(devices, embeddings, group_ids)

    return jax.shard_map(body, mesh=mesh, in_specs=in_specs, out_specs=out_specs, check_vma=False)
```

```python
import jax
import jax.numpy as jnp
from jax import lax
from jax.experimental import pallas as pl
from jax.experimental.pallas import tpu as pltpu
from jax.sharding import PartitionSpec as P

AXES = ("row", "col")
LANES = 128
RADIX = 256


def bit_groups(bits):
    return [b for b in reversed(range(bits)) if b >= 3], [b for b in (1, 2) if b < bits]


def masks_of(group):
    masks = [0]
    for b in group:
        masks += [m | (1 << b) for m in masks]
    return masks[1:]


def swap(devices, mask, held):
    return lax.ppermute(held, AXES, [(i, i ^ mask) for i in range(devices)])


def gather_rows(devices, held):
    far, near = bit_groups(devices.bit_length() - 1)
    for b in far[:-1]:
        held = jnp.concatenate([held, swap(devices, 1 << b | 1, held)], axis=0)
    late = swap(devices, 1 << far[-1] | 1, held)
    parts = [held, late]
    for part in (held, late):
        parts += [swap(devices, m | 1, part) for m in masks_of(near)]
    return jnp.concatenate(parts, axis=0)


def pack(rows_hbm, ids_hbm, out_ref, rows_ref, ids_ref, sems):
    rows, width = rows_ref.shape
    copies = [
        pltpu.make_async_copy(ids_hbm, ids_ref, sems.at[0]),
        pltpu.make_async_copy(rows_hbm, rows_ref, sems.at[1]),
    ]
    for copy in copies:
        copy.start()
    copies[0].wait()
    down = lax.broadcasted_iota(jnp.int32, (rows, rows), 0)
    across = lax.broadcasted_iota(jnp.int32, (rows, rows), 1)
    wide = jnp.broadcast_to(ids_ref[...], (rows, rows))
    ids = jnp.sum(jnp.where(down == across, wide, 0), axis=1, keepdims=True)
    lane = lax.broadcasted_iota(jnp.int32, (rows, LANES), 1)
    low, high = ids & (RADIX - 1), ids >> 8
    coded = jnp.where(lane == 0, low, jnp.where(lane == 1, high, 0))
    out_ref[:, width:] = coded.astype(jnp.float32).astype(jnp.bfloat16)
    copies[1].wait()
    out_ref[:, :width] = rows_ref[...]


def dot_nt(a, b):
    return lax.dot_general(a, b, (((1,), (1,)), ((), ())), preferred_element_type=jnp.float32)


def digits(rows):
    lane = lax.broadcasted_iota(jnp.int32, (rows, LANES), 1)
    return jnp.where(lane == 0, 1.0, jnp.where(lane == 1, float(RADIX), 0.0)).astype(jnp.bfloat16)


def block_stats(width, rows_ref, cols_ref, start, block, own, keep):
    scale = 1.0 / jnp.sqrt(jnp.float32(width))
    cols = cols_ref[pl.ds(start, block), :width]
    col_ids = dot_nt(digits(16), cols_ref[pl.ds(start, block), width:])[:1]
    parts = []
    for first in range(0, rows_ref.shape[0], block):
        s = dot_nt(rows_ref[first : first + block, :width], cols) * scale
        positive = dot_nt(rows_ref[first : first + block, width:], digits(block)) == col_ids
        masked = s
        if rows_ref is cols_ref:
            row_pos = first + lax.broadcasted_iota(jnp.int32, (block, block), 0)
            selfs = row_pos == start + lax.broadcasted_iota(jnp.int32, (block, block), 1)
            positive = jnp.logical_and(positive, jnp.logical_not(selfs))
            masked = jnp.where(selfs, jnp.float32(-1e30), s)
        if first == 0:
            keep(masked[:own], positive[:own])
        top = jnp.max(masked, axis=0, keepdims=True)
        add = jnp.sum(jnp.exp(masked - top), axis=0, keepdims=True)
        possum = jnp.sum(jnp.where(positive, s, 0.0), axis=0, keepdims=True)
        count = jnp.sum(jnp.where(positive, 1.0, 0.0), axis=0, keepdims=True)
        parts.append((top, add, possum, count))
    return merge(parts)


def merge(parts):
    peak = parts[0][0]
    for p in parts[1:]:
        peak = jnp.maximum(peak, p[0])
    added = sum(p[1] * jnp.exp(p[0] - peak) for p in parts)
    return peak, added, sum(p[2] for p in parts), sum(p[3] for p in parts)


def over_blocks(half, block, body, carry):
    if half == block:
        return body(0, carry)
    return lax.fori_loop(
        0, half // block, lambda k, v: body(pl.multiple_of(k * block, block), v), carry
    )


def near_stats(width, own, near_ref, stats_ref, scores_ref, positive_ref):
    half = near_ref.shape[0]
    block = min(half, 256)

    def body(start, carry):
        at = pl.ds(start, block)

        def keep(scores, positive):
            scores_ref[:, at] = scores
            positive_ref[:, at] = jnp.where(positive, 1.0, 0.0)

        stats = block_stats(width, near_ref, near_ref, start, block, own, keep)
        for k, value in enumerate(stats):
            stats_ref[k : k + 1, at] = value
        return carry

    over_blocks(half, block, body, 0)


def loss_and_grad(
    width, own, near_ref, far_ref, stats_ref, near_scores_ref, near_positive_ref,
    loss_ref, grad_ref, lse_ref, inv_ref, scores_ref, positive_ref,
):
    half = near_ref.shape[0]
    total = 2 * half
    block = min(half, 256)
    scale = 1.0 / jnp.sqrt(jnp.float32(width))
    scores_ref[:, :half] = near_scores_ref[...]
    positive_ref[:, :half] = near_positive_ref[...]

    def finish(at, stats, loss):
        peak, added, possum, count = stats
        inverse = 1.0 / count
        lse = peak + jnp.log(added)
        lse_ref[:, at] = lse
        inv_ref[:, at] = inverse
        return loss + jnp.sum(lse - possum * inverse)

    def near_columns(start, loss):
        at = pl.ds(start, block)
        had = tuple(stats_ref[k : k + 1, at] for k in range(4))
        more = block_stats(width, far_ref, near_ref, start, block, own, lambda *_: None)
        return finish(at, merge([had, more]), loss)

    def far_columns(start, loss):
        at = pl.ds(half + start, block)

        def keep(scores, positive):
            scores_ref[:, at] = scores
            positive_ref[:, at] = jnp.where(positive, 1.0, 0.0)

        first = block_stats(width, near_ref, far_ref, start, block, own, keep)
        second = block_stats(width, far_ref, far_ref, start, block, own, lambda *_: None)
        return finish(at, merge([first, second]), loss)

    loss = over_blocks(half, block, far_columns, jnp.float32(0.0))
    loss = over_blocks(half, block, near_columns, loss)
    loss_ref[0] = loss / total

    masked = scores_ref[...]
    positive = positive_ref[...]
    peak = jnp.max(masked, axis=1, keepdims=True)
    lse = peak + jnp.log(jnp.sum(jnp.exp(masked - peak), axis=1, keepdims=True))
    inverse = 1.0 / jnp.sum(positive, axis=1, keepdims=True)
    weight = (jnp.exp(masked - lse) - positive * inverse) / total
    mirrored = (jnp.exp(masked - lse_ref[...]) - positive * inv_ref[...]) / total
    both = jnp.concatenate([weight, mirrored], axis=0).astype(jnp.bfloat16)
    out = jnp.zeros((2 * own, width), jnp.float32)
    for k, ref in enumerate((near_ref, far_ref)):
        out += jnp.dot(
            both[:, k * half : (k + 1) * half], ref[:, :width], preferred_element_type=jnp.float32
        )
    grad_ref[...] = (scale * (out[:own] + out[own:])).astype(jnp.bfloat16)


def on_device(devices, embeddings, group_ids):
    rows, width = embeddings.shape
    total = rows * devices
    half = total // 2
    vmem = pl.BlockSpec(memory_space=pltpu.VMEM)
    params = pltpu.CompilerParams(vmem_limit_bytes=(8 << 20) + 8 * total * width)
    held = pl.pallas_call(
        pack,
        out_shape=jax.ShapeDtypeStruct((rows, width + LANES), jnp.bfloat16),
        in_specs=[pl.BlockSpec(memory_space=pltpu.HBM)] * 2,
        out_specs=vmem,
        scratch_shapes=[
            pltpu.VMEM((rows, width), jnp.bfloat16),
            pltpu.VMEM((1, rows), jnp.int32),
            pltpu.SemaphoreType.DMA((2,)),
        ],
        compiler_params=pltpu.CompilerParams(vmem_limit_bytes=60 << 20),
    )(embeddings, group_ids[None, :])
    near = gather_rows(devices, held)
    far = swap(devices, 1, near)
    stats = pl.pallas_call(
        lambda *refs: near_stats(width, rows, *refs),
        out_shape=(
            jax.ShapeDtypeStruct((4, half), jnp.float32),
            jax.ShapeDtypeStruct((rows, half), jnp.float32),
            jax.ShapeDtypeStruct((rows, half), jnp.float32),
        ),
        in_specs=[vmem],
        out_specs=(vmem, vmem, vmem),
        compiler_params=params,
        cost_estimate=pl.CostEstimate(
            flops=2 * half * half * width, bytes_accessed=2 * half * width, transcendentals=half * half
        ),
    )(near)
    loss, grad = pl.pallas_call(
        lambda *refs: loss_and_grad(width, rows, *refs),
        out_shape=(
            jax.ShapeDtypeStruct((1,), jnp.float32),
            jax.ShapeDtypeStruct((rows, width), jnp.bfloat16),
        ),
        in_specs=[vmem] * 5,
        out_specs=(pl.BlockSpec(memory_space=pltpu.SMEM), vmem),
        scratch_shapes=[
            pltpu.VMEM((1, total), jnp.float32),
            pltpu.VMEM((1, total), jnp.float32),
            pltpu.VMEM((rows, total), jnp.float32),
            pltpu.VMEM((rows, total), jnp.float32),
        ],
        compiler_params=params,
        cost_estimate=pl.CostEstimate(
            flops=6 * half * half * width, bytes_accessed=2 * total * width, transcendentals=3 * half * half
        ),
    )(near, far, *stats)
    return (loss[0], grad)


def solution(mesh):
    in_specs = (P(AXES, None), P(AXES))
    out_specs = (P(), P(AXES, None))
    devices = mesh.shape["row"] * mesh.shape["col"]

    def body(embeddings, group_ids):
        return on_device(devices, embeddings, group_ids)

    return jax.shard_map(body, mesh=mesh, in_specs=in_specs, out_specs=out_specs, check_vma=False)
```

```python
import jax
import jax.numpy as jnp
from jax import lax
from jax.experimental import pallas as pl
from jax.experimental.pallas import tpu as pltpu
from jax.sharding import PartitionSpec as P

AXES = ("row", "col")
LANES = 128
RADIX = 256


def bit_groups(bits):
    return [b for b in reversed(range(bits)) if b >= 3], [b for b in (1, 2) if b < bits]


def masks_of(group):
    masks = [0]
    for b in group:
        masks += [m | (1 << b) for m in masks]
    return masks[1:]


def swap(devices, mask, held):
    return lax.ppermute(held, AXES, [(i, i ^ mask) for i in range(devices)])


def gather_rows(devices, held):
    far, near = bit_groups(devices.bit_length() - 1)
    for b in far[:-1]:
        held = jnp.concatenate([held, swap(devices, 1 << b | 1, held)], axis=0)
    last = 1 << far[-1] | 1
    late = swap(devices, last, held)
    across = swap(devices, 7, held)
    both = jnp.concatenate([held, late], axis=0)
    parts = [both] + [swap(devices, m, both) for m in (3, 5)]
    return jnp.concatenate(parts + [across, swap(devices, last, across)], axis=0)


def pack(rows_hbm, ids_hbm, out_ref, rows_ref, ids_ref, sems):
    rows, width = rows_ref.shape
    copies = [
        pltpu.make_async_copy(ids_hbm, ids_ref, sems.at[0]),
        pltpu.make_async_copy(rows_hbm, rows_ref, sems.at[1]),
    ]
    for copy in copies:
        copy.start()
    copies[0].wait()
    down = lax.broadcasted_iota(jnp.int32, (rows, rows), 0)
    across = lax.broadcasted_iota(jnp.int32, (rows, rows), 1)
    wide = jnp.broadcast_to(ids_ref[...], (rows, rows))
    ids = jnp.sum(jnp.where(down == across, wide, 0), axis=1, keepdims=True)
    lane = lax.broadcasted_iota(jnp.int32, (rows, LANES), 1)
    low, high = ids & (RADIX - 1), ids >> 8
    coded = jnp.where(lane == 0, low, jnp.where(lane == 1, high, 0))
    out_ref[:, width:] = coded.astype(jnp.float32).astype(jnp.bfloat16)
    copies[1].wait()
    out_ref[:, :width] = rows_ref[...]


def dot_nt(a, b):
    return lax.dot_general(a, b, (((1,), (1,)), ((), ())), preferred_element_type=jnp.float32)


def digits(rows):
    lane = lax.broadcasted_iota(jnp.int32, (rows, LANES), 1)
    return jnp.where(lane == 0, 1.0, jnp.where(lane == 1, float(RADIX), 0.0)).astype(jnp.bfloat16)


def block_stats(width, rows_ref, cols_ref, start, block, own, keep):
    scale = 1.0 / jnp.sqrt(jnp.float32(width))
    cols = cols_ref[pl.ds(start, block), :width]
    col_ids = dot_nt(digits(16), cols_ref[pl.ds(start, block), width:])[:1]
    parts = []
    for first in range(0, rows_ref.shape[0], block):
        s = dot_nt(rows_ref[first : first + block, :width], cols) * scale
        positive = dot_nt(rows_ref[first : first + block, width:], digits(block)) == col_ids
        masked = s
        if rows_ref is cols_ref:
            row_pos = first + lax.broadcasted_iota(jnp.int32, (block, block), 0)
            selfs = row_pos == start + lax.broadcasted_iota(jnp.int32, (block, block), 1)
            positive = jnp.logical_and(positive, jnp.logical_not(selfs))
            masked = jnp.where(selfs, jnp.float32(-1e30), s)
        if first == 0:
            keep(masked[:own], positive[:own])
        top = jnp.max(masked, axis=0, keepdims=True)
        add = jnp.sum(jnp.exp(masked - top), axis=0, keepdims=True)
        possum = jnp.sum(jnp.where(positive, s, 0.0), axis=0, keepdims=True)
        count = jnp.sum(jnp.where(positive, 1.0, 0.0), axis=0, keepdims=True)
        parts.append((top, add, possum, count))
    return merge(parts)


def merge(parts):
    peak = parts[0][0]
    for p in parts[1:]:
        peak = jnp.maximum(peak, p[0])
    added = sum(p[1] * jnp.exp(p[0] - peak) for p in parts)
    return peak, added, sum(p[2] for p in parts), sum(p[3] for p in parts)


def over_blocks(half, block, body, carry):
    if half == block:
        return body(0, carry)
    return lax.fori_loop(
        0, half // block, lambda k, v: body(pl.multiple_of(k * block, block), v), carry
    )


def near_stats(width, own, near_ref, stats_ref, scores_ref, positive_ref):
    half = near_ref.shape[0]
    block = min(half, 256)

    def body(start, carry):
        at = pl.ds(start, block)

        def keep(scores, positive):
            scores_ref[:, at] = scores
            positive_ref[:, at] = jnp.where(positive, 1.0, 0.0)

        stats = block_stats(width, near_ref, near_ref, start, block, own, keep)
        for k, value in enumerate(stats):
            stats_ref[k : k + 1, at] = value
        return carry

    over_blocks(half, block, body, 0)


def loss_and_grad(
    width, own, near_ref, far_ref, stats_ref, near_scores_ref, near_positive_ref,
    loss_ref, grad_ref, lse_ref, inv_ref, scores_ref, positive_ref,
):
    half = near_ref.shape[0]
    total = 2 * half
    block = min(half, 256)
    scale = 1.0 / jnp.sqrt(jnp.float32(width))
    scores_ref[:, :half] = near_scores_ref[...]
    positive_ref[:, :half] = near_positive_ref[...]

    def finish(at, stats, loss):
        peak, added, possum, count = stats
        inverse = 1.0 / count
        lse = peak + jnp.log(added)
        lse_ref[:, at] = lse
        inv_ref[:, at] = inverse
        return loss + jnp.sum(lse - possum * inverse)

    def near_columns(start, loss):
        at = pl.ds(start, block)
        had = tuple(stats_ref[k : k + 1, at] for k in range(4))
        more = block_stats(width, far_ref, near_ref, start, block, own, lambda *_: None)
        return finish(at, merge([had, more]), loss)

    def far_columns(start, loss):
        at = pl.ds(half + start, block)

        def keep(scores, positive):
            scores_ref[:, at] = scores
            positive_ref[:, at] = jnp.where(positive, 1.0, 0.0)

        first = block_stats(width, near_ref, far_ref, start, block, own, keep)
        second = block_stats(width, far_ref, far_ref, start, block, own, lambda *_: None)
        return finish(at, merge([first, second]), loss)

    loss = over_blocks(half, block, far_columns, jnp.float32(0.0))
    loss = over_blocks(half, block, near_columns, loss)
    loss_ref[0] = loss / total

    masked = scores_ref[...]
    positive = positive_ref[...]
    peak = jnp.max(masked, axis=1, keepdims=True)
    lse = peak + jnp.log(jnp.sum(jnp.exp(masked - peak), axis=1, keepdims=True))
    inverse = 1.0 / jnp.sum(positive, axis=1, keepdims=True)
    weight = (jnp.exp(masked - lse) - positive * inverse) / total
    mirrored = (jnp.exp(masked - lse_ref[...]) - positive * inv_ref[...]) / total
    both = jnp.concatenate([weight, mirrored], axis=0).astype(jnp.bfloat16)
    out = jnp.zeros((2 * own, width), jnp.float32)
    for k, ref in enumerate((near_ref, far_ref)):
        out += jnp.dot(
            both[:, k * half : (k + 1) * half], ref[:, :width], preferred_element_type=jnp.float32
        )
    grad_ref[...] = (scale * (out[:own] + out[own:])).astype(jnp.bfloat16)


def on_device(devices, embeddings, group_ids):
    rows, width = embeddings.shape
    total = rows * devices
    half = total // 2
    vmem = pl.BlockSpec(memory_space=pltpu.VMEM)
    params = pltpu.CompilerParams(vmem_limit_bytes=(8 << 20) + 8 * total * width)
    held = pl.pallas_call(
        pack,
        out_shape=pltpu.VMEM((rows, width + LANES), jnp.bfloat16),
        in_specs=[pl.BlockSpec(memory_space=pltpu.HBM)] * 2,
        out_specs=vmem,
        scratch_shapes=[
            pltpu.VMEM((rows, width), jnp.bfloat16),
            pltpu.VMEM((1, rows), jnp.int32),
            pltpu.SemaphoreType.DMA((2,)),
        ],
        compiler_params=pltpu.CompilerParams(vmem_limit_bytes=60 << 20),
    )(embeddings, group_ids[None, :])
    near = gather_rows(devices, held)
    far = swap(devices, 1, near)
    stats = pl.pallas_call(
        lambda *refs: near_stats(width, rows, *refs),
        out_shape=(
            jax.ShapeDtypeStruct((4, half), jnp.float32),
            jax.ShapeDtypeStruct((rows, half), jnp.float32),
            jax.ShapeDtypeStruct((rows, half), jnp.float32),
        ),
        in_specs=[vmem],
        out_specs=(vmem, vmem, vmem),
        compiler_params=params,
        cost_estimate=pl.CostEstimate(
            flops=2 * half * half * width, bytes_accessed=2 * half * width, transcendentals=half * half
        ),
    )(near)
    loss, grad = pl.pallas_call(
        lambda *refs: loss_and_grad(width, rows, *refs),
        out_shape=(
            jax.ShapeDtypeStruct((1,), jnp.float32),
            jax.ShapeDtypeStruct((rows, width), jnp.bfloat16),
        ),
        in_specs=[vmem] * 5,
        out_specs=(pl.BlockSpec(memory_space=pltpu.SMEM), vmem),
        scratch_shapes=[
            pltpu.VMEM((1, total), jnp.float32),
            pltpu.VMEM((1, total), jnp.float32),
            pltpu.VMEM((rows, total), jnp.float32),
            pltpu.VMEM((rows, total), jnp.float32),
        ],
        compiler_params=params,
        cost_estimate=pl.CostEstimate(
            flops=6 * half * half * width, bytes_accessed=2 * total * width, transcendentals=3 * half * half
        ),
    )(near, far, *stats)
    return (loss[0], grad)


def solution(mesh):
    in_specs = (P(AXES, None), P(AXES))
    out_specs = (P(), P(AXES, None))
    devices = mesh.shape["row"] * mesh.shape["col"]

    def body(embeddings, group_ids):
        return on_device(devices, embeddings, group_ids)

    return jax.shard_map(body, mesh=mesh, in_specs=in_specs, out_specs=out_specs, check_vma=False)
```

```python
import jax
import jax.numpy as jnp
from jax import lax
from jax.experimental import pallas as pl
from jax.experimental.pallas import tpu as pltpu
from jax.sharding import PartitionSpec as P

AXES = ("row", "col")
LANES = 128
RADIX = 256


def bit_groups(bits):
    return [b for b in reversed(range(bits)) if b >= 3], [b for b in (1, 2) if b < bits]


def masks_of(group):
    masks = [0]
    for b in group:
        masks += [m | (1 << b) for m in masks]
    return masks[1:]


def swap(devices, mask, held):
    return lax.ppermute(held, AXES, [(i, i ^ mask) for i in range(devices)])


def gather_rows(devices, held):
    far, near = bit_groups(devices.bit_length() - 1)
    for b in far[:-1]:
        held = jnp.concatenate([held, swap(devices, 1 << b | 1, held)], axis=0)
    last = 1 << far[-1] | 1
    first, second = (1 << b | 1 for b in near)
    beyond = swap(devices, last, held)
    across = swap(devices, first | second, held)
    held = jnp.concatenate([held, beyond], axis=0)
    one = jnp.concatenate([held, swap(devices, first, held)], axis=0)
    two = swap(devices, second, held)
    two = jnp.concatenate([two, across, swap(devices, last, across)], axis=0)
    other = swap(devices, 1, one)
    return jnp.concatenate([one, other, two], axis=0), swap(devices, 1, two)


def pack(rows_hbm, ids_hbm, out_ref, rows_ref, ids_ref, sems):
    rows, width = rows_ref.shape
    copies = [
        pltpu.make_async_copy(ids_hbm, ids_ref, sems.at[0]),
        pltpu.make_async_copy(rows_hbm, rows_ref, sems.at[1]),
    ]
    for copy in copies:
        copy.start()
    copies[0].wait()
    down = lax.broadcasted_iota(jnp.int32, (rows, rows), 0)
    across = lax.broadcasted_iota(jnp.int32, (rows, rows), 1)
    wide = jnp.broadcast_to(ids_ref[...], (rows, rows))
    ids = jnp.sum(jnp.where(down == across, wide, 0), axis=1, keepdims=True)
    lane = lax.broadcasted_iota(jnp.int32, (rows, LANES), 1)
    low, high = ids & (RADIX - 1), ids >> 8
    coded = jnp.where(lane == 0, low, jnp.where(lane == 1, high, 0))
    out_ref[:, width:] = coded.astype(jnp.float32).astype(jnp.bfloat16)
    copies[1].wait()
    out_ref[:, :width] = rows_ref[...]


def dot_nt(a, b):
    return lax.dot_general(a, b, (((1,), (1,)), ((), ())), preferred_element_type=jnp.float32)


def digits(rows):
    lane = lax.broadcasted_iota(jnp.int32, (rows, LANES), 1)
    return jnp.where(lane == 0, 1.0, jnp.where(lane == 1, float(RADIX), 0.0)).astype(jnp.bfloat16)


def span(rows):
    return rows if rows <= 384 else 256


def block_stats(width, rows_ref, cols_ref, start, own, keep, product=None):
    scale = 1.0 / jnp.sqrt(jnp.float32(width))
    across, down = span(cols_ref.shape[0]), span(rows_ref.shape[0])
    cols = cols_ref[pl.ds(start, across), :width]
    col_ids = dot_nt(digits(16), cols_ref[pl.ds(start, across), width:])[:1]
    parts = []
    for first in range(0, rows_ref.shape[0], down):
        s = dot_nt(rows_ref[first : first + down, :width], cols) if product is None else product
        s = s * scale
        row_ids = dot_nt(rows_ref[first : first + down, width:], digits(LANES))
        positive = jnp.concatenate([row_ids] * (across // LANES), axis=1) == col_ids
        masked = s
        if rows_ref is cols_ref:
            row_pos = first + lax.broadcasted_iota(jnp.int32, (down, across), 0)
            selfs = row_pos == start + lax.broadcasted_iota(jnp.int32, (down, across), 1)
            positive = jnp.logical_and(positive, jnp.logical_not(selfs))
            masked = jnp.where(selfs, jnp.float32(-1e30), s)
        if first == 0:
            keep(masked[:own], positive[:own])
        top = jnp.max(masked, axis=0, keepdims=True)
        add = jnp.sum(jnp.exp(masked - top), axis=0, keepdims=True)
        possum = jnp.sum(jnp.where(positive, s, 0.0), axis=0, keepdims=True)
        count = jnp.sum(jnp.where(positive, 1.0, 0.0), axis=0, keepdims=True)
        parts.append((top, add, possum, count))
    return merge(parts)


def merge(parts):
    peak = parts[0][0]
    for p in parts[1:]:
        peak = jnp.maximum(peak, p[0])
    added = sum(p[1] * jnp.exp(p[0] - peak) for p in parts)
    return peak, added, sum(p[2] for p in parts), sum(p[3] for p in parts)


def over_blocks(rows, body, carry):
    block = span(rows)
    if rows == block:
        return body(0, carry)
    return lax.fori_loop(
        0, rows // block, lambda k, v: body(pl.multiple_of(k * block, block), v), carry
    )


def early_stats(width, own, early_ref, stats_ref, scores_ref, positive_ref):
    early = early_ref.shape[0]

    def body(start, carry):
        at = pl.ds(start, span(early))

        def keep(scores, positive):
            scores_ref[:, at] = scores
            positive_ref[:, at] = jnp.where(positive, 1.0, 0.0)

        stats = block_stats(width, early_ref, early_ref, start, own, keep)
        for k, value in enumerate(stats):
            stats_ref[k : k + 1, at] = value
        return carry

    over_blocks(early, body, 0)


def loss_and_grad(
    width, own, early_ref, late_ref, stats_ref, early_scores_ref, early_positive_ref,
    loss_hbm, grad_hbm, lse_ref, inv_ref, scores_ref, positive_ref, loss_ref, grad_ref, sems,
):
    early, late = early_ref.shape[0], late_ref.shape[0]
    total = early + late
    scale = 1.0 / jnp.sqrt(jnp.float32(width))
    scores_ref[:, :early] = early_scores_ref[...]
    positive_ref[:, :early] = early_positive_ref[...]

    def finish(at, stats, loss):
        peak, added, possum, count = stats
        inverse = 1.0 / count
        lse = peak + jnp.log(added)
        lse_ref[:, at] = lse
        inv_ref[:, at] = inverse
        return loss + jnp.sum(lse - possum * inverse)

    def early_columns(start, loss):
        at = pl.ds(start, span(early))
        had = tuple(stats_ref[k : k + 1, at] for k in range(4))
        turned = None if product is None else product.T
        more = block_stats(width, late_ref, early_ref, start, own, lambda *_: None, turned)
        return finish(at, merge([had, more]), loss)

    def late_columns(start, loss):
        at = pl.ds(early + start, span(late))

        def keep(scores, positive):
            scores_ref[:, at] = scores
            positive_ref[:, at] = jnp.where(positive, 1.0, 0.0)

        first = block_stats(width, early_ref, late_ref, start, own, keep, product)
        second = block_stats(width, late_ref, late_ref, start, own, lambda *_: None)
        return finish(at, merge([first, second]), loss)

    product = None
    if span(early) == early and span(late) == late:
        product = dot_nt(early_ref[:, :width], late_ref[:, :width])
    loss = over_blocks(late, late_columns, jnp.float32(0.0))
    loss = over_blocks(early, early_columns, loss)
    loss_ref[...] = jnp.full((1, 1), loss / total)
    copies = [pltpu.make_async_copy(loss_ref, loss_hbm, sems.at[0])]
    copies[0].start()

    masked = scores_ref[...]
    positive = positive_ref[...]
    peak = jnp.max(masked, axis=1, keepdims=True)
    lse = peak + jnp.log(jnp.sum(jnp.exp(masked - peak), axis=1, keepdims=True))
    inverse = 1.0 / jnp.sum(positive, axis=1, keepdims=True)
    weight = (jnp.exp(masked - lse) - positive * inverse) / total
    mirrored = (jnp.exp(masked - lse_ref[...]) - positive * inv_ref[...]) / total
    both = jnp.concatenate([weight, mirrored], axis=0).astype(jnp.bfloat16)
    parts = 2
    for k in range(parts):
        at = pl.ds(k * width // parts, width // parts)
        out = jnp.dot(both[:, :early], early_ref[:, at], preferred_element_type=jnp.float32)
        out += jnp.dot(both[:, early:], late_ref[:, at], preferred_element_type=jnp.float32)
        grad_ref[:, at] = (scale * (out[:own] + out[own:])).astype(jnp.bfloat16)
        copies.append(
            pltpu.make_async_copy(grad_ref.at[:, at], grad_hbm.at[:, at], sems.at[1 + k])
        )
        copies[-1].start()
    for copy in copies:
        copy.wait()


def on_device(devices, embeddings, group_ids):
    rows, width = embeddings.shape
    total = rows * devices
    vmem = pl.BlockSpec(memory_space=pltpu.VMEM)
    params = pltpu.CompilerParams(vmem_limit_bytes=(8 << 20) + 8 * total * width)
    held = pl.pallas_call(
        pack,
        out_shape=pltpu.VMEM((rows, width + LANES), jnp.bfloat16),
        in_specs=[pl.BlockSpec(memory_space=pltpu.HBM)] * 2,
        out_specs=vmem,
        scratch_shapes=[
            pltpu.VMEM((rows, width), jnp.bfloat16),
            pltpu.VMEM((1, rows), jnp.int32),
            pltpu.SemaphoreType.DMA((2,)),
        ],
        compiler_params=pltpu.CompilerParams(vmem_limit_bytes=60 << 20),
    )(embeddings, group_ids[None, :])
    early_rows, late_rows = gather_rows(devices, held)
    early, late = early_rows.shape[0], late_rows.shape[0]
    stats = pl.pallas_call(
        lambda *refs: early_stats(width, rows, *refs),
        out_shape=(
            jax.ShapeDtypeStruct((4, early), jnp.float32),
            jax.ShapeDtypeStruct((rows, early), jnp.float32),
            jax.ShapeDtypeStruct((rows, early), jnp.float32),
        ),
        in_specs=[vmem],
        out_specs=(vmem, vmem, vmem),
        compiler_params=params,
        cost_estimate=pl.CostEstimate(
            flops=2 * early * early * width, bytes_accessed=2 * early * width, transcendentals=early * early
        ),
    )(early_rows)
    loss, grad = pl.pallas_call(
        lambda *refs: loss_and_grad(width, rows, *refs),
        out_shape=(
            jax.ShapeDtypeStruct((1, 1), jnp.float32),
            jax.ShapeDtypeStruct((rows, width), jnp.bfloat16),
        ),
        in_specs=[vmem] * 5,
        out_specs=[pl.BlockSpec(memory_space=pltpu.HBM)] * 2,
        scratch_shapes=[
            pltpu.VMEM((1, total), jnp.float32),
            pltpu.VMEM((1, total), jnp.float32),
            pltpu.VMEM((rows, total), jnp.float32),
            pltpu.VMEM((rows, total), jnp.float32),
            pltpu.VMEM((1, 1), jnp.float32),
            pltpu.VMEM((rows, width), jnp.bfloat16),
            pltpu.SemaphoreType.DMA((3,)),
        ],
        compiler_params=params,
        cost_estimate=pl.CostEstimate(
            flops=4 * total * late * width, bytes_accessed=2 * total * width, transcendentals=2 * total * late
        ),
    )(early_rows, late_rows, *stats)
    return (loss[0, 0], grad)


def solution(mesh):
    in_specs = (P(AXES, None), P(AXES))
    out_specs = (P(), P(AXES, None))
    devices = mesh.shape["row"] * mesh.shape["col"]

    def body(embeddings, group_ids):
        return on_device(devices, embeddings, group_ids)

    return jax.shard_map(body, mesh=mesh, in_specs=in_specs, out_specs=out_specs, check_vma=False)
```

```python
import jax
import jax.numpy as jnp
from jax import lax
from jax.experimental import pallas as pl
from jax.experimental.pallas import tpu as pltpu
from jax.sharding import PartitionSpec as P

AXES = ("row", "col")
LANES = 128
RADIX = 256


def bit_groups(bits):
    return [b for b in reversed(range(bits)) if b >= 3], [b for b in (1, 2) if b < bits]


def masks_of(group):
    masks = [0]
    for b in group:
        masks += [m | (1 << b) for m in masks]
    return masks[1:]


def swap(devices, mask, held):
    return lax.ppermute(held, AXES, [(i, i ^ mask) for i in range(devices)])


def rotate(devices, bits, back, held):
    low, high = (1 << b for b in bits)
    after = {0: low, low: low | high, low | high: high, high: 0}
    pairs = [(i, i & ~(low | high) | after[i & (low | high)]) for i in range(devices)]
    pairs = [(i ^ 1, j) for i, j in pairs]
    return lax.ppermute(held, AXES, [(j, i) if back else (i, j) for i, j in pairs])


def gather_rows(devices, held):
    far, near = bit_groups(devices.bit_length() - 1)
    for b in far[:-1]:
        held = jnp.concatenate([held, swap(devices, 1 << b | 1, held)], axis=0)
    last = 1 << far[-1] | 1
    beyond = swap(devices, last, held)
    across = swap(devices, sum(1 << b for b in near), held)
    held = jnp.concatenate([held, beyond], axis=0)
    one = jnp.concatenate([held, rotate(devices, near, False, held)], axis=0)
    two = rotate(devices, near, True, held)
    two = jnp.concatenate([two, across, swap(devices, last, across)], axis=0)
    other = swap(devices, 1, one)
    return jnp.concatenate([one, other, two], axis=0), swap(devices, 1, two)


def pack(rows_hbm, ids_hbm, out_ref, ids_ref, sems):
    rows, width = rows_hbm.shape
    copies = [
        pltpu.make_async_copy(ids_hbm, ids_ref, sems.at[0]),
        pltpu.make_async_copy(rows_hbm, out_ref.at[:, :width], sems.at[1]),
    ]
    for copy in copies:
        copy.start()
    copies[0].wait()
    down = lax.broadcasted_iota(jnp.int32, (rows, rows), 0)
    across = lax.broadcasted_iota(jnp.int32, (rows, rows), 1)
    wide = jnp.broadcast_to(ids_ref[...], (rows, rows))
    ids = jnp.sum(jnp.where(down == across, wide, 0), axis=1, keepdims=True)
    lane = lax.broadcasted_iota(jnp.int32, (rows, LANES), 1)
    low, high = ids & (RADIX - 1), ids >> 8
    coded = jnp.where(lane == 0, low, jnp.where(lane == 1, high, 0))
    out_ref[:, width:] = coded.astype(jnp.float32).astype(jnp.bfloat16)
    copies[1].wait()


def dot_nt(a, b):
    return lax.dot_general(a, b, (((1,), (1,)), ((), ())), preferred_element_type=jnp.float32)


def digits(rows):
    lane = lax.broadcasted_iota(jnp.int32, (rows, LANES), 1)
    return jnp.where(lane == 0, 1.0, jnp.where(lane == 1, float(RADIX), 0.0)).astype(jnp.bfloat16)


def span(rows):
    return rows if rows <= 384 else 256


def block_stats(width, rows_ref, cols_ref, start, own, keep, products=None):
    scale = 1.0 / jnp.sqrt(jnp.float32(width))
    across, down = span(cols_ref.shape[0]), span(rows_ref.shape[0])
    if products is not None:
        down, across = products[0].shape
    cols = cols_ref[pl.ds(start, across), :width]
    col_ids = dot_nt(digits(16), cols_ref[pl.ds(start, across), width:])[:1]
    parts = []
    for first in range(0, rows_ref.shape[0], down):
        if products is None:
            s = dot_nt(rows_ref[first : first + down, :width], cols) * scale
        else:
            s = products[first // down] * scale
        row_ids = dot_nt(rows_ref[first : first + down, width:], digits(LANES))
        positive = jnp.concatenate([row_ids] * (across // LANES), axis=1) == col_ids
        masked = s
        if rows_ref is cols_ref:
            row_pos = first + lax.broadcasted_iota(jnp.int32, (down, across), 0)
            selfs = row_pos == start + lax.broadcasted_iota(jnp.int32, (down, across), 1)
            positive = jnp.logical_and(positive, jnp.logical_not(selfs))
            masked = jnp.where(selfs, jnp.float32(-1e30), s)
        if first == 0:
            keep(masked[:own], positive[:own])
        top = jnp.max(masked, axis=0, keepdims=True)
        add = jnp.sum(jnp.exp(masked - top), axis=0, keepdims=True)
        possum = jnp.sum(jnp.where(positive, s, 0.0), axis=0, keepdims=True)
        count = jnp.sum(jnp.where(positive, 1.0, 0.0), axis=0, keepdims=True)
        parts.append((top, add, possum, count))
    return merge(parts)


def merge(parts):
    peak = parts[0][0]
    for p in parts[1:]:
        peak = jnp.maximum(peak, p[0])
    added = sum(p[1] * jnp.exp(p[0] - peak) for p in parts)
    return peak, added, sum(p[2] for p in parts), sum(p[3] for p in parts)


def over_blocks(rows, body, carry):
    block = span(rows)
    if rows == block:
        return body(0, carry)
    return lax.fori_loop(
        0, rows // block, lambda k, v: body(pl.multiple_of(k * block, block), v), carry
    )


def early_stats(width, own, early_ref, stats_ref, scores_ref, positive_ref):
    early = early_ref.shape[0]

    def body(start, carry):
        at = pl.ds(start, span(early))

        def keep(scores, positive):
            scores_ref[:, at] = scores
            positive_ref[:, at] = jnp.where(positive, 1.0, 0.0)

        stats = block_stats(width, early_ref, early_ref, start, own, keep)
        for k, value in enumerate(stats):
            stats_ref[k : k + 1, at] = value
        return carry

    over_blocks(early, body, 0)


def loss_and_grad(
    width, own, early_ref, late_ref, stats_ref, early_scores_ref, early_positive_ref,
    loss_hbm, grad_hbm, lse_ref, inv_ref, scores_ref, positive_ref, loss_ref, grad_ref, sems,
):
    early, late = early_ref.shape[0], late_ref.shape[0]
    total = early + late
    scale = 1.0 / jnp.sqrt(jnp.float32(width))
    scores_ref[:, :early] = early_scores_ref[...]
    positive_ref[:, :early] = early_positive_ref[...]

    def finish(at, stats, loss):
        peak, added, possum, count = stats
        inverse = 1.0 / count
        lse = peak + jnp.log(added)
        lse_ref[:, at] = lse
        inv_ref[:, at] = inverse
        return loss + jnp.sum(lse - possum * inverse)

    def early_columns(start, loss, products=None):
        at = pl.ds(start, span(early) if products is None else products[0].shape[1])
        had = tuple(stats_ref[k : k + 1, at] for k in range(4))
        more = block_stats(width, late_ref, early_ref, start, own, lambda *_: None, products)
        return finish(at, merge([had, more]), loss)

    def late_columns(start, loss):
        at = pl.ds(early + start, span(late))

        def keep(scores, positive):
            scores_ref[:, at] = scores
            positive_ref[:, at] = jnp.where(positive, 1.0, 0.0)

        first = block_stats(width, early_ref, late_ref, start, own, keep, products)
        second = block_stats(width, late_ref, late_ref, start, own, lambda *_: None)
        return finish(at, merge([first, second]), loss)

    products = None
    if span(early) == early and span(late) == late:
        products = [
            dot_nt(early_ref[k : k + LANES, :width], late_ref[:, :width])
            for k in range(0, early, LANES)
        ]
    loss = over_blocks(late, late_columns, jnp.float32(0.0))
    if products is None:
        loss = over_blocks(early, early_columns, loss)
    else:
        for k, product in enumerate(products):
            loss = early_columns(k * LANES, loss, [product.T])
    loss_ref[...] = jnp.full((1, 1), loss / total)
    copies = [pltpu.make_async_copy(loss_ref, loss_hbm, sems.at[0])]
    copies[0].start()

    masked = scores_ref[...]
    positive = positive_ref[...]
    peak = jnp.max(masked, axis=1, keepdims=True)
    lse = peak + jnp.log(jnp.sum(jnp.exp(masked - peak), axis=1, keepdims=True))
    inverse = 1.0 / jnp.sum(positive, axis=1, keepdims=True)
    weight = (jnp.exp(masked - lse) - positive * inverse) / total
    mirrored = (jnp.exp(masked - lse_ref[...]) - positive * inv_ref[...]) / total
    both = jnp.concatenate([weight, mirrored], axis=0).astype(jnp.bfloat16)
    parts = 2
    for k in range(parts):
        at = pl.ds(k * width // parts, width // parts)
        out = jnp.dot(both[:, :early], early_ref[:, at], preferred_element_type=jnp.float32)
        out += jnp.dot(both[:, early:], late_ref[:, at], preferred_element_type=jnp.float32)
        grad_ref[:, at] = (scale * (out[:own] + out[own:])).astype(jnp.bfloat16)
        copies.append(
            pltpu.make_async_copy(grad_ref.at[:, at], grad_hbm.at[:, at], sems.at[1 + k])
        )
        copies[-1].start()
    for copy in copies:
        copy.wait()


def on_device(devices, embeddings, group_ids):
    rows, width = embeddings.shape
    total = rows * devices
    vmem = pl.BlockSpec(memory_space=pltpu.VMEM)
    params = pltpu.CompilerParams(vmem_limit_bytes=(8 << 20) + 8 * total * width)
    held = pl.pallas_call(
        pack,
        out_shape=pltpu.VMEM((rows, width + LANES), jnp.bfloat16),
        in_specs=[pl.BlockSpec(memory_space=pltpu.HBM)] * 2,
        out_specs=vmem,
        scratch_shapes=[
            pltpu.VMEM((1, rows), jnp.int32),
            pltpu.SemaphoreType.DMA((2,)),
        ],
        compiler_params=pltpu.CompilerParams(vmem_limit_bytes=60 << 20),
    )(embeddings, group_ids[None, :])
    early_rows, late_rows = gather_rows(devices, held)
    early, late = early_rows.shape[0], late_rows.shape[0]
    stats = pl.pallas_call(
        lambda *refs: early_stats(width, rows, *refs),
        out_shape=(
            jax.ShapeDtypeStruct((4, early), jnp.float32),
            jax.ShapeDtypeStruct((rows, early), jnp.float32),
            jax.ShapeDtypeStruct((rows, early), jnp.float32),
        ),
        in_specs=[vmem],
        out_specs=(vmem, vmem, vmem),
        compiler_params=params,
        cost_estimate=pl.CostEstimate(
            flops=2 * early * early * width, bytes_accessed=2 * early * width, transcendentals=early * early
        ),
    )(early_rows)
    loss, grad = pl.pallas_call(
        lambda *refs: loss_and_grad(width, rows, *refs),
        out_shape=(
            jax.ShapeDtypeStruct((1, 1), jnp.float32),
            jax.ShapeDtypeStruct((rows, width), jnp.bfloat16),
        ),
        in_specs=[vmem] * 5,
        out_specs=[pl.BlockSpec(memory_space=pltpu.HBM)] * 2,
        scratch_shapes=[
            pltpu.VMEM((1, total), jnp.float32),
            pltpu.VMEM((1, total), jnp.float32),
            pltpu.VMEM((rows, total), jnp.float32),
            pltpu.VMEM((rows, total), jnp.float32),
            pltpu.VMEM((1, 1), jnp.float32),
            pltpu.VMEM((rows, width), jnp.bfloat16),
            pltpu.SemaphoreType.DMA((3,)),
        ],
        compiler_params=params,
        cost_estimate=pl.CostEstimate(
            flops=4 * total * late * width, bytes_accessed=2 * total * width, transcendentals=2 * total * late
        ),
    )(early_rows, late_rows, *stats)
    return (loss[0, 0], grad)


def solution(mesh):
    in_specs = (P(AXES, None), P(AXES))
    out_specs = (P(), P(AXES, None))
    devices = mesh.shape["row"] * mesh.shape["col"]

    def body(embeddings, group_ids):
        return on_device(devices, embeddings, group_ids)

    return jax.shard_map(body, mesh=mesh, in_specs=in_specs, out_specs=out_specs, check_vma=False)
```

```python
import jax
import jax.numpy as jnp
from jax import lax
from jax.experimental import pallas as pl
from jax.experimental.pallas import tpu as pltpu
from jax.sharding import PartitionSpec as P

AXES = ("row", "col")
LANES = 128
RADIX = 256
LOG2E = 1.4426950408889634


def bit_groups(bits):
    return [b for b in reversed(range(bits)) if b >= 3], [b for b in (1, 2) if b < bits]


def masks_of(group):
    masks = [0]
    for b in group:
        masks += [m | (1 << b) for m in masks]
    return masks[1:]


def swap(devices, mask, held):
    return lax.ppermute(held, AXES, [(i, i ^ mask) for i in range(devices)])


def rotate(devices, bits, back, held):
    low, high = (1 << b for b in bits)
    after = {0: low, low: low | high, low | high: high, high: 0}
    pairs = [(i, i & ~(low | high) | after[i & (low | high)]) for i in range(devices)]
    pairs = [(i ^ 1, j) for i, j in pairs]
    ahead = {i: j for i, j in pairs}
    behind = {j: i for i, j in pairs}
    turned = [(i, (ahead if (i & 1) == back else behind)[i]) for i in range(devices)]
    return lax.ppermute(held, AXES, turned)


def gather_rows(devices, held):
    far, near = bit_groups(devices.bit_length() - 1)
    for b in far[:-1]:
        held = jnp.concatenate([held, swap(devices, 1 << b | 1, held)], axis=0)
    last = 1 << far[-1] | 1
    beyond = swap(devices, last, held)
    across = swap(devices, sum(1 << b for b in near), held)
    held = jnp.concatenate([held, beyond], axis=0)
    one = jnp.concatenate([held, rotate(devices, near, False, held)], axis=0)
    two = rotate(devices, near, True, held)
    two = jnp.concatenate([two, across, swap(devices, last, across)], axis=0)
    half = swap(devices, 1, one)
    rest = swap(devices, 1, two)
    return jnp.concatenate([one, two], axis=0), half, rest


def pack(rows_hbm, ids_hbm, out_ref, ids_ref, sems):
    rows, width = rows_hbm.shape
    copies = [
        pltpu.make_async_copy(ids_hbm, ids_ref, sems.at[0]),
        pltpu.make_async_copy(rows_hbm, out_ref.at[:, :width], sems.at[1]),
    ]
    for copy in copies:
        copy.start()
    copies[0].wait()
    down = lax.broadcasted_iota(jnp.int32, (rows, rows), 0)
    across = lax.broadcasted_iota(jnp.int32, (rows, rows), 1)
    wide = jnp.broadcast_to(ids_ref[...], (rows, rows))
    ids = jnp.sum(jnp.where(down == across, wide, 0), axis=1, keepdims=True)
    lane = lax.broadcasted_iota(jnp.int32, (rows, LANES), 1)
    low, high = ids & (RADIX - 1), ids >> 8
    coded = jnp.where(lane == 0, low, jnp.where(lane == 1, high, 0))
    out_ref[:, width:] = coded.astype(jnp.float32).astype(jnp.bfloat16)
    copies[1].wait()


def dot_nt(a, b):
    return lax.dot_general(a, b, (((1,), (1,)), ((), ())), preferred_element_type=jnp.float32)


def digits(rows):
    lane = lax.broadcasted_iota(jnp.int32, (rows, LANES), 1)
    return jnp.where(lane == 0, 1.0, jnp.where(lane == 1, float(RADIX), 0.0)).astype(jnp.bfloat16)


def span(rows):
    return rows if rows <= 384 else 256


def block_stats(width, rows_ref, cols_ref, start, own, keep, products=None, weigh=1):
    across, down = span(cols_ref.shape[0]), span(rows_ref.shape[0])
    if products is not None:
        down, across = products[0].shape
    cols = cols_ref[pl.ds(start, across), :width]
    col_ids = dot_nt(digits(16), cols_ref[pl.ds(start, across), width:])[:1]
    parts = []
    for first in range(0, rows_ref.shape[0], down):
        if products is None:
            s = dot_nt(rows_ref[first : first + down, :width], cols)
        else:
            s = products[first // down]
        row_ids = dot_nt(rows_ref[first : first + down, width:], digits(LANES))
        positive = jnp.concatenate([row_ids] * (across // LANES), axis=1) == col_ids
        masked = s
        if rows_ref is cols_ref:
            row_pos = first + lax.broadcasted_iota(jnp.int32, (down, across), 0)
            selfs = row_pos == start + lax.broadcasted_iota(jnp.int32, (down, across), 1)
            positive = jnp.logical_and(positive, jnp.logical_not(selfs))
            masked = jnp.where(selfs, jnp.float32(-1e30), s)
        if first == 0:
            keep(masked[:own], positive[:own])
        top = jnp.max(masked, axis=0, keepdims=True)
        add = jnp.sum(power(masked - top, width), axis=0, keepdims=True)
        possum = jnp.zeros_like(top)
        if weigh:
            possum = weigh * jnp.sum(jnp.where(positive, s, 0.0), axis=0, keepdims=True)
        count = jnp.sum(jnp.where(positive, 1.0, 0.0), axis=0, keepdims=True)
        parts.append((top, add, possum, count))
    return merge(parts, width)


def power(raw, width):
    return jnp.exp2(raw * (LOG2E / jnp.sqrt(jnp.float32(width))))


def merge(parts, width):
    peak = parts[0][0]
    for p in parts[1:]:
        peak = jnp.maximum(peak, p[0])
    added = sum(p[1] * power(p[0] - peak, width) for p in parts)
    return peak, added, sum(p[2] for p in parts), sum(p[3] for p in parts)


def over_blocks(rows, body, carry):
    block = span(rows)
    if rows == block:
        return body(0, carry)
    return lax.fori_loop(
        0, rows // block, lambda k, v: body(pl.multiple_of(k * block, block), v), carry
    )


def keep_in(scores_ref, positive_ref, at):
    def keep(scores, positive):
        scores_ref[:, at] = scores
        positive_ref[:, at] = jnp.where(positive, 1.0, 0.0)

    return keep


def near_stats(width, own, near_ref, stats_ref, scores_ref, positive_ref):
    near = near_ref.shape[0]

    def body(start, carry):
        at = pl.ds(start, span(near))
        keep = keep_in(scores_ref, positive_ref, at)
        stats = block_stats(width, near_ref, near_ref, start, own, keep)
        for k, value in enumerate(stats):
            stats_ref[k : k + 1, at] = value
        return carry

    over_blocks(near, body, 0)


def extend(width, own, early_ref, late_ref, had, scores_ref, positive_ref, emit, carry):
    early, late = early_ref.shape[0], late_ref.shape[0]
    had_stats, had_scores, had_positive = had
    scores_ref[:, :early] = had_scores[...]
    positive_ref[:, :early] = had_positive[...]

    def early_columns(start, carry, products=None):
        at = pl.ds(start, span(early) if products is None else products[0].shape[1])
        first = tuple(had_stats[k : k + 1, at] for k in range(4))
        more = block_stats(width, late_ref, early_ref, start, own, lambda *_: None, products, 0)
        return emit(at, merge([first, more], width), carry)

    def late_columns(start, carry):
        at = pl.ds(early + start, span(late))
        keep = keep_in(scores_ref, positive_ref, at)
        first = block_stats(width, early_ref, late_ref, start, own, keep, products, 2)
        second = block_stats(width, late_ref, late_ref, start, own, lambda *_: None)
        return emit(at, merge([first, second], width), carry)

    products = None
    if span(early) == early and span(late) == late:
        products = [
            dot_nt(early_ref[k : k + LANES, :width], late_ref[:, :width])
            for k in range(0, early, LANES)
        ]
    carry = over_blocks(late, late_columns, carry)
    if products is None:
        return over_blocks(early, early_columns, carry)
    for k, product in enumerate(products):
        carry = early_columns(k * LANES, carry, [product.T])
    return carry


def more_stats(
    width, own, early_ref, late_ref, had_stats, had_scores, had_positive,
    stats_ref, scores_ref, positive_ref,
):
    def emit(at, stats, carry):
        for k, value in enumerate(stats):
            stats_ref[k : k + 1, at] = value
        return carry

    had = (had_stats, had_scores, had_positive)
    extend(width, own, early_ref, late_ref, had, scores_ref, positive_ref, emit, 0)


def loss_and_grad(
    width, own, early_ref, late_ref, had_stats, had_scores, had_positive,
    loss_hbm, grad_hbm, lse_ref, inv_ref, scores_ref, positive_ref, loss_ref, grad_ref, sems,
):
    early, late = early_ref.shape[0], late_ref.shape[0]
    total = early + late
    scale = 1.0 / jnp.sqrt(jnp.float32(width))

    def emit(at, stats, loss):
        peak, added, possum, count = stats
        inverse = 1.0 / count
        lse = scale * peak + jnp.log(added)
        lse_ref[:, at] = lse
        inv_ref[:, at] = inverse
        return loss + jnp.sum(lse - scale * possum * inverse)

    had = (had_stats, had_scores, had_positive)
    loss = extend(
        width, own, early_ref, late_ref, had, scores_ref, positive_ref, emit, jnp.float32(0.0)
    )
    loss_ref[...] = jnp.full((1, 1), loss / total)
    copies = [pltpu.make_async_copy(loss_ref, loss_hbm, sems.at[0])]
    copies[0].start()

    masked = scores_ref[...] * scale
    positive = positive_ref[...]
    peak = jnp.max(masked, axis=1, keepdims=True)
    lse = peak + jnp.log(jnp.sum(jnp.exp(masked - peak), axis=1, keepdims=True))
    inverse = 1.0 / jnp.sum(positive, axis=1, keepdims=True)
    weight = (jnp.exp(masked - lse) - positive * inverse) / total
    mirrored = (jnp.exp(masked - lse_ref[...]) - positive * inv_ref[...]) / total
    both = jnp.concatenate([weight, mirrored], axis=0).astype(jnp.bfloat16)
    parts = 2
    for k in range(parts):
        at = pl.ds(k * width // parts, width // parts)
        out = jnp.dot(both[:, :early], early_ref[:, at], preferred_element_type=jnp.float32)
        out += jnp.dot(both[:, early:], late_ref[:, at], preferred_element_type=jnp.float32)
        grad_ref[:, at] = (scale * (out[:own] + out[own:])).astype(jnp.bfloat16)
        copies.append(
            pltpu.make_async_copy(grad_ref.at[:, at], grad_hbm.at[:, at], sems.at[1 + k])
        )
        copies[-1].start()
    for copy in copies:
        copy.wait()


def on_device(devices, embeddings, group_ids):
    rows, width = embeddings.shape
    total = rows * devices
    vmem = pl.BlockSpec(memory_space=pltpu.VMEM)
    params = pltpu.CompilerParams(vmem_limit_bytes=(8 << 20) + 8 * total * width)
    held = pl.pallas_call(
        pack,
        out_shape=pltpu.VMEM((rows, width + LANES), jnp.bfloat16),
        in_specs=[pl.BlockSpec(memory_space=pltpu.HBM)] * 2,
        out_specs=vmem,
        scratch_shapes=[
            pltpu.VMEM((1, rows), jnp.int32),
            pltpu.SemaphoreType.DMA((2,)),
        ],
        compiler_params=pltpu.CompilerParams(vmem_limit_bytes=60 << 20),
    )(embeddings, group_ids[None, :])
    near, half, rest = gather_rows(devices, held)

    def stats_shape(columns):
        return tuple(jax.ShapeDtypeStruct((k, columns), jnp.float32) for k in (4, rows, rows))

    def cost(products):
        return pl.CostEstimate(
            flops=2 * products * width, bytes_accessed=2 * total * width, transcendentals=products
        )

    first = near.shape[0]
    stats = pl.pallas_call(
        lambda *refs: near_stats(width, rows, *refs),
        out_shape=stats_shape(first),
        in_specs=[vmem],
        out_specs=(vmem, vmem, vmem),
        compiler_params=params,
        cost_estimate=cost(first * first),
    )(near)
    early = first + half.shape[0]
    stats = pl.pallas_call(
        lambda *refs: more_stats(width, rows, *refs),
        out_shape=stats_shape(early),
        in_specs=[vmem] * 5,
        out_specs=(vmem, vmem, vmem),
        compiler_params=params,
        cost_estimate=cost(early * early - first * first),
    )(near, half, *stats)
    early_rows = jnp.concatenate([near, half], axis=0)
    loss, grad = pl.pallas_call(
        lambda *refs: loss_and_grad(width, rows, *refs),
        out_shape=(
            jax.ShapeDtypeStruct((1, 1), jnp.float32),
            jax.ShapeDtypeStruct((rows, width), jnp.bfloat16),
        ),
        in_specs=[vmem] * 5,
        out_specs=[pl.BlockSpec(memory_space=pltpu.HBM)] * 2,
        scratch_shapes=[
            pltpu.VMEM((1, total), jnp.float32),
            pltpu.VMEM((1, total), jnp.float32),
            pltpu.VMEM((rows, total), jnp.float32),
            pltpu.VMEM((rows, total), jnp.float32),
            pltpu.VMEM((1, 1), jnp.float32),
            pltpu.VMEM((rows, width), jnp.bfloat16),
            pltpu.SemaphoreType.DMA((3,)),
        ],
        compiler_params=params,
        cost_estimate=cost(total * total - early * early),
    )(early_rows, rest, *stats)
    return (loss[0, 0], grad)


def solution(mesh):
    in_specs = (P(AXES, None), P(AXES))
    out_specs = (P(), P(AXES, None))
    devices = mesh.shape["row"] * mesh.shape["col"]

    def body(embeddings, group_ids):
        return on_device(devices, embeddings, group_ids)

    return jax.shard_map(body, mesh=mesh, in_specs=in_specs, out_specs=out_specs, check_vma=False)
```

```python
import jax
import jax.numpy as jnp
from jax import lax
from jax.experimental import pallas as pl
from jax.experimental.pallas import tpu as pltpu
from jax.sharding import PartitionSpec as P

AXES = ("row", "col")
LANES = 128
RADIX = 256
LOG2E = 1.4426950408889634


def bit_groups(bits):
    return [b for b in reversed(range(bits)) if b >= 3], [b for b in (1, 2) if b < bits]


def masks_of(group):
    masks = [0]
    for b in group:
        masks += [m | (1 << b) for m in masks]
    return masks[1:]


def swap(devices, mask, held):
    return lax.ppermute(held, AXES, [(i, i ^ mask) for i in range(devices)])


def rotate(devices, bits, back, held):
    low, high = (1 << b for b in bits)
    after = {0: low, low: low | high, low | high: high, high: 0}
    pairs = [(i, i & ~(low | high) | after[i & (low | high)]) for i in range(devices)]
    pairs = [(i ^ 1, j) for i, j in pairs]
    ahead = {i: j for i, j in pairs}
    behind = {j: i for i, j in pairs}
    turned = [(i, (ahead if (i & 1) == back else behind)[i]) for i in range(devices)]
    return lax.ppermute(held, AXES, turned)


def gather_rows(devices, held):
    far, near = bit_groups(devices.bit_length() - 1)
    for b in far[:-1]:
        held = jnp.concatenate([held, swap(devices, 1 << b | 1, held)], axis=0)
    last = 1 << far[-1] | 1
    beyond = swap(devices, last, held)
    across = swap(devices, sum(1 << b for b in near), held)
    held = jnp.concatenate([held, beyond], axis=0)
    one = jnp.concatenate([held, rotate(devices, near, False, held)], axis=0)
    two = rotate(devices, near, True, held)
    two = jnp.concatenate([two, across, swap(devices, last, across)], axis=0)
    half = swap(devices, 1, one)
    rest = swap(devices, 1, two)
    return jnp.concatenate([one, two], axis=0), half, rest


def pack(rows_hbm, ids_hbm, out_ref, ids_ref, sems):
    rows, width = rows_hbm.shape
    copies = [
        pltpu.make_async_copy(ids_hbm, ids_ref, sems.at[0]),
        pltpu.make_async_copy(rows_hbm, out_ref.at[:, :width], sems.at[1]),
    ]
    for copy in copies:
        copy.start()
    copies[0].wait()
    down = lax.broadcasted_iota(jnp.int32, (rows, rows), 0)
    across = lax.broadcasted_iota(jnp.int32, (rows, rows), 1)
    wide = jnp.broadcast_to(ids_ref[...], (rows, rows))
    ids = jnp.sum(jnp.where(down == across, wide, 0), axis=1, keepdims=True)
    lane = lax.broadcasted_iota(jnp.int32, (rows, LANES), 1)
    low, high = ids & (RADIX - 1), ids >> 8
    coded = jnp.where(lane == 0, low, jnp.where(lane == 1, high, 0))
    out_ref[:, width:] = coded.astype(jnp.float32).astype(jnp.bfloat16)
    copies[1].wait()


def dot_nt(a, b):
    return lax.dot_general(a, b, (((1,), (1,)), ((), ())), preferred_element_type=jnp.float32)


def digits(rows):
    lane = lax.broadcasted_iota(jnp.int32, (rows, LANES), 1)
    return jnp.where(lane == 0, 1.0, jnp.where(lane == 1, float(RADIX), 0.0)).astype(jnp.bfloat16)


def span(rows):
    return rows if rows <= 384 else 256


def block_stats(width, rows_ref, cols_ref, start, own, keep, products=None):
    across, down = span(cols_ref.shape[0]), span(rows_ref.shape[0])
    if products is not None:
        down, across = products[0].shape
    cols = cols_ref[pl.ds(start, across), :width]
    col_ids = dot_nt(digits(16), cols_ref[pl.ds(start, across), width:])[:1]
    parts = []
    for first in range(0, rows_ref.shape[0], down):
        if products is None:
            s = dot_nt(rows_ref[first : first + down, :width], cols)
        else:
            s = products[first // down]
        row_ids = dot_nt(rows_ref[first : first + down, width:], digits(LANES))
        positive = jnp.concatenate([row_ids] * (across // LANES), axis=1) == col_ids
        masked = s
        if rows_ref is cols_ref:
            row_pos = first + lax.broadcasted_iota(jnp.int32, (down, across), 0)
            selfs = row_pos == start + lax.broadcasted_iota(jnp.int32, (down, across), 1)
            positive = jnp.logical_and(positive, jnp.logical_not(selfs))
            masked = jnp.where(selfs, jnp.float32(-1e30), s)
        if first == 0:
            keep(masked[:own], positive[:own])
        top = jnp.max(masked, axis=0, keepdims=True)
        add = jnp.sum(power(masked - top, width), axis=0, keepdims=True)
        possum = jnp.sum(jnp.where(positive, s, 0.0), axis=0, keepdims=True)
        count = jnp.sum(jnp.where(positive, 1.0, 0.0), axis=0, keepdims=True)
        parts.append((top, add, possum, count))
    return merge(parts, width)


def power(raw, width):
    return jnp.exp2(raw * (LOG2E / jnp.sqrt(jnp.float32(width))))


def merge(parts, width):
    peak = parts[0][0]
    for p in parts[1:]:
        peak = jnp.maximum(peak, p[0])
    added = sum(p[1] * power(p[0] - peak, width) for p in parts)
    return peak, added, sum(p[2] for p in parts), sum(p[3] for p in parts)


def over_blocks(rows, body, carry):
    block = span(rows)
    if rows == block:
        return body(0, carry)
    return lax.fori_loop(
        0, rows // block, lambda k, v: body(pl.multiple_of(k * block, block), v), carry
    )


def keep_in(scores_ref, positive_ref, at):
    def keep(scores, positive):
        scores_ref[:, at] = scores
        positive_ref[:, at] = jnp.where(positive, 1.0, 0.0)

    return keep


def near_stats(width, own, near_ref, stats_ref, scores_ref, positive_ref):
    near = near_ref.shape[0]

    def body(start, carry):
        at = pl.ds(start, span(near))
        keep = keep_in(scores_ref, positive_ref, at)
        stats = block_stats(width, near_ref, near_ref, start, own, keep)
        for k, value in enumerate(stats):
            stats_ref[k : k + 1, at] = value
        return carry

    over_blocks(near, body, 0)


def extend(width, own, early_ref, late_ref, had, scores_ref, positive_ref, emit, carry):
    early, late = early_ref.shape[0], late_ref.shape[0]
    had_stats, had_scores, had_positive = had
    scores_ref[:, :early] = had_scores[...]
    positive_ref[:, :early] = had_positive[...]

    def early_columns(start, carry, products=None):
        at = pl.ds(start, span(early) if products is None else products[0].shape[1])
        first = tuple(had_stats[k : k + 1, at] for k in range(4))
        more = block_stats(width, late_ref, early_ref, start, own, lambda *_: None, products)
        return emit(at, merge([first, more], width), carry)

    def late_columns(start, carry):
        at = pl.ds(early + start, span(late))
        keep = keep_in(scores_ref, positive_ref, at)
        first = block_stats(width, early_ref, late_ref, start, own, keep, products)
        second = block_stats(width, late_ref, late_ref, start, own, lambda *_: None)
        return emit(at, merge([first, second], width), carry)

    products = None
    if span(early) == early and span(late) == late:
        products = [
            dot_nt(early_ref[k : k + LANES, :width], late_ref[:, :width])
            for k in range(0, early, LANES)
        ]
    carry = over_blocks(late, late_columns, carry)
    if products is None:
        return over_blocks(early, early_columns, carry)
    for k, product in enumerate(products):
        carry = early_columns(k * LANES, carry, [product.T])
    return carry


def more_stats(
    width, own, early_ref, late_ref, had_stats, had_scores, had_positive,
    stats_ref, scores_ref, positive_ref,
):
    def emit(at, stats, carry):
        for k, value in enumerate(stats):
            stats_ref[k : k + 1, at] = value
        return carry

    had = (had_stats, had_scores, had_positive)
    extend(width, own, early_ref, late_ref, had, scores_ref, positive_ref, emit, 0)


def loss_and_grad(
    width, own, early_ref, late_ref, had_stats, had_scores, had_positive,
    loss_hbm, grad_hbm, lse_ref, inv_ref, scores_ref, positive_ref, loss_ref, grad_ref, sems,
):
    early, late = early_ref.shape[0], late_ref.shape[0]
    total = early + late
    scale = 1.0 / jnp.sqrt(jnp.float32(width))

    def emit(at, stats, loss):
        peak, added, possum, count = stats
        inverse = 1.0 / count
        lse = scale * peak + jnp.log(added)
        lse_ref[:, at] = lse
        inv_ref[:, at] = inverse
        return loss + jnp.sum(lse - scale * possum * inverse)

    had = (had_stats, had_scores, had_positive)
    loss = extend(
        width, own, early_ref, late_ref, had, scores_ref, positive_ref, emit, jnp.float32(0.0)
    )
    loss_ref[...] = jnp.full((1, 1), loss / total)
    copies = [pltpu.make_async_copy(loss_ref, loss_hbm, sems.at[0])]
    copies[0].start()

    masked = scores_ref[...] * scale
    positive = positive_ref[...]
    peak = jnp.max(masked, axis=1, keepdims=True)
    lse = peak + jnp.log(jnp.sum(jnp.exp(masked - peak), axis=1, keepdims=True))
    inverse = 1.0 / jnp.sum(positive, axis=1, keepdims=True)
    weight = (jnp.exp(masked - lse) - positive * inverse) / total
    mirrored = (jnp.exp(masked - lse_ref[...]) - positive * inv_ref[...]) / total
    both = jnp.concatenate([weight, mirrored], axis=0).astype(jnp.bfloat16)
    parts = 2
    for k in range(parts):
        at = pl.ds(k * width // parts, width // parts)
        out = jnp.dot(both[:, :early], early_ref[:, at], preferred_element_type=jnp.float32)
        out += jnp.dot(both[:, early:], late_ref[:, at], preferred_element_type=jnp.float32)
        grad_ref[:, at] = (scale * (out[:own] + out[own:])).astype(jnp.bfloat16)
        copies.append(
            pltpu.make_async_copy(grad_ref.at[:, at], grad_hbm.at[:, at], sems.at[1 + k])
        )
        copies[-1].start()
    for copy in copies:
        copy.wait()


def on_device(devices, embeddings, group_ids):
    rows, width = embeddings.shape
    total = rows * devices
    vmem = pl.BlockSpec(memory_space=pltpu.VMEM)
    params = pltpu.CompilerParams(vmem_limit_bytes=(8 << 20) + 8 * total * width)
    held = pl.pallas_call(
        pack,
        out_shape=pltpu.VMEM((rows, width + LANES), jnp.bfloat16),
        in_specs=[pl.BlockSpec(memory_space=pltpu.HBM)] * 2,
        out_specs=vmem,
        scratch_shapes=[
            pltpu.VMEM((1, rows), jnp.int32),
            pltpu.SemaphoreType.DMA((2,)),
        ],
        compiler_params=pltpu.CompilerParams(vmem_limit_bytes=60 << 20),
    )(embeddings, group_ids[None, :])
    near, half, rest = gather_rows(devices, held)

    def stats_shape(columns):
        return tuple(jax.ShapeDtypeStruct((k, columns), jnp.float32) for k in (4, rows, rows))

    def cost(products):
        return pl.CostEstimate(
            flops=2 * products * width, bytes_accessed=2 * total * width, transcendentals=products
        )

    first = near.shape[0]
    stats = pl.pallas_call(
        lambda *refs: near_stats(width, rows, *refs),
        out_shape=stats_shape(first),
        in_specs=[vmem],
        out_specs=(vmem, vmem, vmem),
        compiler_params=params,
        cost_estimate=cost(first * first),
    )(near)
    early = first + half.shape[0]
    stats = pl.pallas_call(
        lambda *refs: more_stats(width, rows, *refs),
        out_shape=stats_shape(early),
        in_specs=[vmem] * 5,
        out_specs=(vmem, vmem, vmem),
        compiler_params=params,
        cost_estimate=cost(early * early - first * first),
    )(near, half, *stats)
    early_rows = jnp.concatenate([near, half], axis=0)
    loss, grad = pl.pallas_call(
        lambda *refs: loss_and_grad(width, rows, *refs),
        out_shape=(
            jax.ShapeDtypeStruct((1, 1), jnp.float32),
            jax.ShapeDtypeStruct((rows, width), jnp.bfloat16),
        ),
        in_specs=[vmem] * 5,
        out_specs=[pl.BlockSpec(memory_space=pltpu.HBM)] * 2,
        scratch_shapes=[
            pltpu.VMEM((1, total), jnp.float32),
            pltpu.VMEM((1, total), jnp.float32),
            pltpu.VMEM((rows, total), jnp.float32),
            pltpu.VMEM((rows, total), jnp.float32),
            pltpu.VMEM((1, 1), jnp.float32),
            pltpu.VMEM((rows, width), jnp.bfloat16),
            pltpu.SemaphoreType.DMA((3,)),
        ],
        compiler_params=params,
        cost_estimate=cost(total * total - early * early),
    )(early_rows, rest, *stats)
    return (loss[0, 0], grad)


def solution(mesh):
    in_specs = (P(AXES, None), P(AXES))
    out_specs = (P(), P(AXES, None))
    devices = mesh.shape["row"] * mesh.shape["col"]

    def body(embeddings, group_ids):
        return on_device(devices, embeddings, group_ids)

    return jax.shard_map(body, mesh=mesh, in_specs=in_specs, out_specs=out_specs, check_vma=False)
```

```python
import jax
import jax.numpy as jnp
from jax import lax
from jax.experimental import pallas as pl
from jax.experimental.pallas import tpu as pltpu
from jax.sharding import PartitionSpec as P

AXES = ("row", "col")
LANES = 128
RADIX = 256
LOG2E = 1.4426950408889634


def bit_groups(bits):
    return [b for b in reversed(range(bits)) if b >= 3], [b for b in (1, 2) if b < bits]


def masks_of(group):
    masks = [0]
    for b in group:
        masks += [m | (1 << b) for m in masks]
    return masks[1:]


def swap(devices, mask, held):
    return lax.ppermute(held, AXES, [(i, i ^ mask) for i in range(devices)])


def rotate(devices, bits, back, held):
    low, high = (1 << b for b in bits)
    after = {0: low, low: low | high, low | high: high, high: 0}
    pairs = [(i, i & ~(low | high) | after[i & (low | high)]) for i in range(devices)]
    pairs = [(i ^ 1, j) for i, j in pairs]
    ahead = {i: j for i, j in pairs}
    behind = {j: i for i, j in pairs}
    turned = [(i, (ahead if (i & 1) == back else behind)[i]) for i in range(devices)]
    return lax.ppermute(held, AXES, turned)


def gather_rows(devices, held):
    far, near = bit_groups(devices.bit_length() - 1)
    for b in far[:-1]:
        held = jnp.concatenate([held, swap(devices, 1 << b | 1, held)], axis=0)
    last = 1 << far[-1] | 1
    beyond = swap(devices, last, held)
    across = swap(devices, sum(1 << b for b in near), held)
    held = jnp.concatenate([held, beyond], axis=0)
    one = jnp.concatenate([held, rotate(devices, near, False, held)], axis=0)
    two = rotate(devices, near, True, held)
    two = jnp.concatenate([two, across, swap(devices, last, across)], axis=0)
    half = swap(devices, 1, one)
    rest = swap(devices, 1, two)
    return jnp.concatenate([one, two], axis=0), half, rest


def pack(rows_hbm, ids_hbm, out_ref, ids_ref, sems):
    rows, width = rows_hbm.shape
    copies = [
        pltpu.make_async_copy(ids_hbm, ids_ref, sems.at[0]),
        pltpu.make_async_copy(rows_hbm, out_ref.at[:, :width], sems.at[1]),
    ]
    for copy in copies:
        copy.start()
    copies[0].wait()
    down = lax.broadcasted_iota(jnp.int32, (rows, rows), 0)
    across = lax.broadcasted_iota(jnp.int32, (rows, rows), 1)
    wide = jnp.broadcast_to(ids_ref[...], (rows, rows))
    ids = jnp.sum(jnp.where(down == across, wide, 0), axis=1, keepdims=True)
    lane = lax.broadcasted_iota(jnp.int32, (rows, LANES), 1)
    low, high = ids & (RADIX - 1), ids >> 8
    coded = jnp.where(lane == 0, low, jnp.where(lane == 1, high, 0))
    out_ref[:, width:] = coded.astype(jnp.float32).astype(jnp.bfloat16)
    copies[1].wait()


def dot_nt(a, b):
    return lax.dot_general(a, b, (((1,), (1,)), ((), ())), preferred_element_type=jnp.float32)


def digits(rows):
    lane = lax.broadcasted_iota(jnp.int32, (rows, LANES), 1)
    return jnp.where(lane == 0, 1.0, jnp.where(lane == 1, float(RADIX), 0.0)).astype(jnp.bfloat16)


def span(rows):
    return rows if rows <= 384 else 256


def block_stats(width, rows_ref, cols_ref, start, own, keep, products=None):
    across, down = span(cols_ref.shape[0]), span(rows_ref.shape[0])
    if products is not None:
        down, across = products[0].shape
    cols = cols_ref[pl.ds(start, across), :width]
    col_ids = dot_nt(digits(16), cols_ref[pl.ds(start, across), width:])[:1]
    parts = []
    for first in range(0, rows_ref.shape[0], down):
        if products is None:
            s = dot_nt(rows_ref[first : first + down, :width], cols)
        else:
            s = products[first // down]
        row_ids = dot_nt(rows_ref[first : first + down, width:], digits(LANES))
        positive = jnp.concatenate([row_ids] * (across // LANES), axis=1) == col_ids
        masked = s
        if rows_ref is cols_ref:
            row_pos = first + lax.broadcasted_iota(jnp.int32, (down, across), 0)
            selfs = row_pos == start + lax.broadcasted_iota(jnp.int32, (down, across), 1)
            positive = jnp.logical_and(positive, jnp.logical_not(selfs))
            masked = jnp.where(selfs, jnp.float32(-1e30), s)
        if first == 0:
            keep(masked[:own], positive[:own])
        top = jnp.max(masked, axis=0, keepdims=True)
        add = jnp.sum(power(masked - top, width), axis=0, keepdims=True)
        possum = jnp.sum(jnp.where(positive, s, 0.0), axis=0, keepdims=True)
        count = jnp.sum(jnp.where(positive, 1.0, 0.0), axis=0, keepdims=True)
        parts.append((top, add, possum, count))
    return merge(parts, width)


def power(raw, width):
    return jnp.exp2(raw * (LOG2E / jnp.sqrt(jnp.float32(width))))


def merge(parts, width):
    peak = parts[0][0]
    for p in parts[1:]:
        peak = jnp.maximum(peak, p[0])
    added = sum(p[1] * power(p[0] - peak, width) for p in parts)
    return peak, added, sum(p[2] for p in parts), sum(p[3] for p in parts)


def over_blocks(rows, body, carry):
    block = span(rows)
    if rows == block:
        return body(0, carry)
    return lax.fori_loop(
        0, rows // block, lambda k, v: body(pl.multiple_of(k * block, block), v), carry
    )


def keep_in(scores_ref, positive_ref, at):
    def keep(scores, positive):
        scores_ref[:, at] = scores
        positive_ref[:, at] = jnp.where(positive, 1.0, 0.0)

    return keep


def near_stats(width, own, near_ref, stats_ref, scores_ref, positive_ref):
    near = near_ref.shape[0]

    def body(start, carry):
        at = pl.ds(start, span(near))
        keep = keep_in(scores_ref, positive_ref, at)
        stats = block_stats(width, near_ref, near_ref, start, own, keep)
        for k, value in enumerate(stats):
            stats_ref[k : k + 1, at] = value
        return carry

    over_blocks(near, body, 0)


def extend(width, own, early_ref, late_ref, had, scores_ref, positive_ref, emit, carry):
    early, late = early_ref.shape[0], late_ref.shape[0]
    had_stats, had_scores, had_positive = had
    scores_ref[:, :early] = had_scores[...]
    positive_ref[:, :early] = had_positive[...]

    def early_columns(start, carry, products=None):
        at = pl.ds(start, span(early) if products is None else products[0].shape[1])
        first = tuple(had_stats[k : k + 1, at] for k in range(4))
        more = block_stats(width, late_ref, early_ref, start, own, lambda *_: None, products)
        return emit(at, merge([first, more], width), carry)

    def late_columns(start, carry):
        at = pl.ds(early + start, span(late))
        keep = keep_in(scores_ref, positive_ref, at)
        first = block_stats(width, early_ref, late_ref, start, own, keep, products)
        second = block_stats(width, late_ref, late_ref, start, own, lambda *_: None)
        return emit(at, merge([first, second], width), carry)

    products = None
    if span(early) == early and span(late) == late:
        products = [
            dot_nt(early_ref[k : k + LANES, :width], late_ref[:, :width])
            for k in range(0, early, LANES)
        ]
    carry = over_blocks(late, late_columns, carry)
    if products is None:
        return over_blocks(early, early_columns, carry)
    for k, product in enumerate(products):
        carry = early_columns(k * LANES, carry, [product.T])
    return carry


def more_stats(
    width, own, early_ref, late_ref, had_stats, had_scores, had_positive,
    stats_ref, scores_ref, positive_ref,
):
    def emit(at, stats, carry):
        for k, value in enumerate(stats):
            stats_ref[k : k + 1, at] = value
        return carry

    had = (had_stats, had_scores, had_positive)
    extend(width, own, early_ref, late_ref, had, scores_ref, positive_ref, emit, 0)


def loss_and_grad(
    width, own, early_ref, late_ref, had_stats, had_scores, had_positive,
    loss_hbm, grad_hbm, lse_ref, inv_ref, scores_ref, positive_ref, loss_ref, grad_ref, sems,
):
    early, late = early_ref.shape[0], late_ref.shape[0]
    total = early + late
    scale = 1.0 / jnp.sqrt(jnp.float32(width))

    def emit(at, stats, loss):
        peak, added, possum, count = stats
        inverse = 1.0 / count
        lse = scale * peak + jnp.log(added)
        lse_ref[:, at] = lse
        inv_ref[:, at] = inverse
        return loss + jnp.sum(lse - scale * possum * inverse)

    had = (had_stats, had_scores, had_positive)
    loss = extend(
        width, own, early_ref, late_ref, had, scores_ref, positive_ref, emit, jnp.float32(0.0)
    )
    loss_ref[...] = jnp.full((1, 1), loss / total)
    copies = [pltpu.make_async_copy(loss_ref, loss_hbm, sems.at[0])]
    copies[0].start()

    masked = scores_ref[...] * scale
    positive = positive_ref[...]
    peak = jnp.max(masked, axis=1, keepdims=True)
    lse = peak + jnp.log(jnp.sum(jnp.exp(masked - peak), axis=1, keepdims=True))
    inverse = 1.0 / jnp.sum(positive, axis=1, keepdims=True)
    weight = (jnp.exp(masked - lse) - positive * inverse) / total
    mirrored = (jnp.exp(masked - lse_ref[...]) - positive * inv_ref[...]) / total
    both = jnp.concatenate([weight, mirrored], axis=0).astype(jnp.bfloat16)
    parts = 4
    for k in range(parts):
        at = pl.ds(k * width // parts, width // parts)
        out = jnp.dot(both[:, :early], early_ref[:, at], preferred_element_type=jnp.float32)
        out += jnp.dot(both[:, early:], late_ref[:, at], preferred_element_type=jnp.float32)
        grad_ref[:, at] = (scale * (out[:own] + out[own:])).astype(jnp.bfloat16)
        copies.append(
            pltpu.make_async_copy(grad_ref.at[:, at], grad_hbm.at[:, at], sems.at[1 + k])
        )
        copies[-1].start()
    for copy in copies:
        copy.wait()


def on_device(devices, embeddings, group_ids):
    rows, width = embeddings.shape
    total = rows * devices
    vmem = pl.BlockSpec(memory_space=pltpu.VMEM)
    params = pltpu.CompilerParams(vmem_limit_bytes=(8 << 20) + 8 * total * width)
    held = pl.pallas_call(
        pack,
        out_shape=pltpu.VMEM((rows, width + LANES), jnp.bfloat16),
        in_specs=[pl.BlockSpec(memory_space=pltpu.HBM)] * 2,
        out_specs=vmem,
        scratch_shapes=[
            pltpu.VMEM((1, rows), jnp.int32),
            pltpu.SemaphoreType.DMA((2,)),
        ],
        compiler_params=pltpu.CompilerParams(vmem_limit_bytes=60 << 20),
    )(embeddings, group_ids[None, :])
    near, half, rest = gather_rows(devices, held)

    def stats_shape(columns):
        return tuple(jax.ShapeDtypeStruct((k, columns), jnp.float32) for k in (4, rows, rows))

    def cost(products):
        return pl.CostEstimate(
            flops=2 * products * width, bytes_accessed=2 * total * width, transcendentals=products
        )

    first = near.shape[0]
    stats = pl.pallas_call(
        lambda *refs: near_stats(width, rows, *refs),
        out_shape=stats_shape(first),
        in_specs=[vmem],
        out_specs=(vmem, vmem, vmem),
        compiler_params=params,
        cost_estimate=cost(first * first),
    )(near)
    early = first + half.shape[0]
    stats = pl.pallas_call(
        lambda *refs: more_stats(width, rows, *refs),
        out_shape=stats_shape(early),
        in_specs=[vmem] * 5,
        out_specs=(vmem, vmem, vmem),
        compiler_params=params,
        cost_estimate=cost(early * early - first * first),
    )(near, half, *stats)
    early_rows = jnp.concatenate([near, half], axis=0)
    loss, grad = pl.pallas_call(
        lambda *refs: loss_and_grad(width, rows, *refs),
        out_shape=(
            jax.ShapeDtypeStruct((1, 1), jnp.float32),
            jax.ShapeDtypeStruct((rows, width), jnp.bfloat16),
        ),
        in_specs=[vmem] * 5,
        out_specs=[pl.BlockSpec(memory_space=pltpu.HBM)] * 2,
        scratch_shapes=[
            pltpu.VMEM((1, total), jnp.float32),
            pltpu.VMEM((1, total), jnp.float32),
            pltpu.VMEM((rows, total), jnp.float32),
            pltpu.VMEM((rows, total), jnp.float32),
            pltpu.VMEM((1, 1), jnp.float32),
            pltpu.VMEM((rows, width), jnp.bfloat16),
            pltpu.SemaphoreType.DMA((5,)),
        ],
        compiler_params=params,
        cost_estimate=cost(total * total - early * early),
    )(early_rows, rest, *stats)
    return (loss[0, 0], grad)


def solution(mesh):
    in_specs = (P(AXES, None), P(AXES))
    out_specs = (P(), P(AXES, None))
    devices = mesh.shape["row"] * mesh.shape["col"]

    def body(embeddings, group_ids):
        return on_device(devices, embeddings, group_ids)

    return jax.shard_map(body, mesh=mesh, in_specs=in_specs, out_specs=out_specs, check_vma=False)
```
